32 devices in a mesh: cols: 8 (over z, x), sec: 4 (over y, core).
Axes of the slice: x: 2, y: 2, z: 4, core: 2. Of those that a mesh axis runs over, the one named last changes fastest.
Arguments:
- trial: float32 [16, 16, 96, 512], P('cols', None, None, 'sec'), may hold values from -6 to 6
- orbitals: float32 [8, 16, 96, 512], P('cols', None, None, 'sec'), may hold values from -6 to 6
- potential: float32 [16, 96, 512], P(None, None, 'sec'), may hold values from -4 to 4
- owner: int32 [2], replicated, may hold values from 0 to 7
Outputs:
- response: float32 [16, 16, 96, 512], P('cols', None, None, 'sec')
The draws below stay inside these ranges and needn't reach their ends.
All inputs are finite; a program needn't handle non-finite values.
Results may differ from the reference program's by a relative error of at most 0.00002.
Values sent between devices are 32-bit elements; how exact they have to be, the bound alone decides.
No kernel may reach another device: no remote copies, remote signals or barrier semaphores. Data moves between devices by JAX's collectives and lax.ppermute only.
A program may use at most 64 MiB of HBM per device.

```python
import jax
import jax.numpy as jnp
from jax import lax

NY = 16
NZ = 96
ROUNDS = 2
COLUMNS = 16
SLOTS = 8
NX = 512
N_COLS = 8


def levels(own_key, extent, shards, low, largest):
    loudness = 1.0
    for position, shards_of in shards:
        heights = jax.random.uniform(jax.random.fold_in(jax.random.fold_in(own_key, 6), position), (shards_of,), jnp.float32, low / len(shards), largest / len(shards))
        loudness = loudness * jnp.repeat(jnp.exp(heights), extent[position] // shards_of).reshape((-1,) + (1,) * (len(extent) - 1 - position))
    return loudness


def centred(stream_key, shape, width, bound, split=(), kind=jnp.bfloat16):
    factor_of = levels(stream_key, shape, split, -0.22, 0.18) if split else 1.0
    array = jax.random.normal(stream_key, shape, jnp.float32) * width * factor_of
    return jnp.minimum(jnp.maximum(array, -bound), bound).astype(kind)


def setup_inputs(seed: int = 0) -> dict:
    keys = jax.random.split(jax.random.key(seed), 5)
    return {
        "trial": centred(keys[0], (COLUMNS, NY, NZ, NX), 1.0, 6.0, ((0, 8), (3, 4)), jnp.float32),
        "orbitals": centred(keys[1], (SLOTS, NY, NZ, NX), 1.0, 6.0, ((0, 8), (3, 4)), jnp.float32),
        "potential": jnp.clip(jax.random.uniform(keys[2], (NY, NZ, NX), jnp.float32, -4.0, 4.0) * levels(keys[2], (NY, NZ, NX), ((2, 4),), -0.4, 0.0), -4.0, 4.0),
        "owner": jax.random.randint(keys[3], (ROUNDS,), 0, N_COLS).astype(jnp.int32),
    }


grid_step = 0.5
spectrum_mid = 16.0
spectrum_half = 20.0
occupation = 2.0
weight_zero = 0.4
weight_one = -0.5
weight_two = 0.3
weight_three = -0.25


def apply_scaled(extended, potential):
    center = extended[..., 2:-2]
    diag_coef = -30.0 / 12.0
    near_coef = 16.0 / 12.0
    far_coef = -1.0 / 12.0
    along_x = diag_coef * center + near_coef * (extended[..., 3:-1] + extended[..., 1:-3]) + far_coef * (extended[..., 4:] + extended[..., :-4])
    leading = center.ndim - 3
    padded = jnp.pad(center, [(0, 0)] * leading + [(2, 2), (2, 2), (0, 0)])
    along_y = diag_coef * center + near_coef * (padded[..., 3:-1, 2:-2, :] + padded[..., 1:-3, 2:-2, :]) + far_coef * (padded[..., 4:, 2:-2, :] + padded[..., :-4, 2:-2, :])
    along_z = diag_coef * center + near_coef * (padded[..., 2:-2, 3:-1, :] + padded[..., 2:-2, 1:-3, :]) + far_coef * (padded[..., 2:-2, 4:, :] + padded[..., 2:-2, :-4, :])
    kinetic = -0.5 * (along_x + along_y + along_z) / (grid_step * grid_step)
    return (kinetic + potential * center - spectrum_mid * center) / spectrum_half


def wrapped(field):
    return jnp.concatenate([field[..., -2:], field, field[..., :2]], axis=-1)


def reference(trial, orbitals, potential, owner):
    def one_column(column):
        total = jnp.zeros_like(column)
        for turn in range(ROUNDS):
            orbital = orbitals[owner[turn]]
            first = orbital * column
            second = apply_scaled(wrapped(first), potential)
            third = 2.0 * apply_scaled(wrapped(second), potential) - first
            fourth = 2.0 * apply_scaled(wrapped(third), potential) - second
            filtered = weight_zero * first + weight_one * second + weight_two * third + weight_three * fourth
            total = total + occupation * orbital * filtered
        return total

    return lax.map(one_column, trial)
```

```python
import functools

import jax
import jax.numpy as jnp
from jax import lax
from jax.experimental import pallas as pl
from jax.experimental.pallas import tpu as pltpu
from jax.sharding import PartitionSpec as P

SCALE = 120.0
ALPHA = 0.6 * SCALE
BETA = 0.25 * SCALE**2
GAMMA = 0.1 * SCALE**3
FINAL = -2.0 / SCALE**3
HALO = 6
ZP = 8
CHUNK = 32


def lanes(rows):
    return lax.broadcasted_iota(jnp.int32, (rows, 128), 1)


def between(lane, low, high):
    return (lane >= low) & (lane < high)


def pack_edges(plane, ny, lane, first):
    tile = jnp.zeros_like(plane(0))
    for y in range(ny):
        source = 0 if first else 128 - HALO
        moved = pltpu.roll(plane(y), (8 * y - source) % 128, 1)
        tile = jnp.where(between(lane, 8 * y, 8 * y + HALO), moved, tile)
    return tile


def halo_plane(left, right, low, high, lane, y):
    inner = lane % 64
    tile = jnp.where(inner < 6, pltpu.roll(left, (-8 * y) % 128, 1), 0.0)
    tile = jnp.where(between(inner, 22, 28), pltpu.roll(right, (22 - 8 * y) % 128, 1), tile)
    tile = jnp.where(between(lane, 6, 12), pltpu.roll(low, 6, 1), tile)
    tile = jnp.where(between(lane, 16, 22), pltpu.roll(low, 22, 1), tile)
    tile = jnp.where(between(lane, 70, 76), pltpu.roll(high, 70, 1), tile)
    tile = jnp.where(between(lane, 80, 86), pltpu.roll(high, 86, 1), tile)
    return tile


def pack_kernel(trial, potential, last, first):
    columns, ny, nz, _ = trial.shape
    lane = lanes(nz)
    for out, leading in ((last, False), (first, True)):
        for c in range(columns):
            out[c] = pack_edges(lambda y: trial[c, y], ny, lane, leading)
        out[columns] = pack_edges(lambda y: potential[y], ny, lane, leading)


def prepare_kernel(trial, potential, left, right, trial_halo, scaled, scaled_halo):
    columns, ny, nz, _ = trial.shape
    lane = lanes(nz)
    half = ny // 2
    for y in range(half):
        tile = jnp.zeros((nz, 128), jnp.float32)
        for c in range(columns):
            part = halo_plane(left[c], right[c], trial[c, y], trial[c, y + half], lane, y)
            tile = tile + (pltpu.roll(part, 32 * c, 1) if c else part)
        trial_halo[y] = tile
        part = halo_plane(left[columns], right[columns], potential[y], potential[y + half], lane, y)
        scaled_halo[y] = 6.0 * (part + pltpu.roll(part, 32, 1)) - 8.0
    for y in range(ny):
        scaled[y] = 6.0 * potential[y] - 8.0


def gather_kernel(count, rows, where, *refs):
    blocks, (whole, last, first) = refs[:count], refs[count:]
    nz = last.shape[0]
    ny = whole.shape[0] // nz
    for k in range(count):
        whole[pl.ds(pl.multiple_of(where[k] * rows, 8), rows), :] = blocks[k][...]
    lane = lanes(nz)
    last[...] = pack_edges(lambda y: whole[y * nz : (y + 1) * nz], ny, lane, False)
    first[...] = pack_edges(lambda y: whole[y * nz : (y + 1) * nz], ny, lane, True)


def clear_borders(ref, ny, nz):
    for c in range(ref.shape[0]):
        for y in (0, 1, ny + 2, ny + 3):
            ref[c, y] = jnp.zeros_like(ref[c, y])

        @pl.loop(2, ny + 2)
        def _(y):
            ref[c, y, 0:ZP] = jnp.zeros((ZP, 128), jnp.float32)
            ref[c, y, ZP + nz : 2 * ZP + nz] = jnp.zeros((ZP, 128), jnp.float32)


def neighbours(ref, c, y, at, rows):
    near = (ref[c, y - 1, pl.ds(at, rows)] + ref[c, y + 1, pl.ds(at, rows)]) + (
        ref[c, y, pl.ds(at - 1, rows)] + ref[c, y, pl.ds(at + 1, rows)]
    )
    far = (ref[c, y - 2, pl.ds(at, rows)] + ref[c, y + 2, pl.ds(at, rows)]) + (
        ref[c, y, pl.ds(at - 2, rows)] + ref[c, y, pl.ds(at + 2, rows)]
    )
    return near, far


def wrap_halo(ref, half, nz, lane):
    inside = pl.ds(ZP, nz)
    for k in range(2):
        ref[0, half + 2 + k, inside] = jnp.where(lane < 64, pltpu.roll(ref[0, 2 + k, inside], 64, 1), 0.0)
        ref[0, k, inside] = jnp.where(lane >= 64, pltpu.roll(ref[0, half + k, inside], 64, 1), 0.0)


def round_kernel(adds, psi, left, right, trial, trial_halo, scaled, scaled_halo, *refs):
    if adds:
        total, out, w, u, v, ends, w_halo, u_halo, v_halo = refs
    else:
        out, w, u, v, ends, w_halo, u_halo, v_halo = refs
    columns, ny, nz, _ = trial.shape
    half = ny // 2
    full = lanes(nz)
    lane = lanes(CHUNK)
    for ref in (w, u, v):
        clear_borders(ref, ny, nz)
    for ref in (w_halo, u_halo, v_halo):
        clear_borders(ref, half, nz)

    for y in range(half):
        part = halo_plane(left[...], right[...], psi[y], psi[y + half], full, y)
        w_halo[0, y + 2, pl.ds(ZP, nz)] = (part + pltpu.roll(part, 32, 1)) * trial_halo[y]
    wrap_halo(w_halo, half, nz, full)

    @pl.loop(0, ny)
    def _(y):
        for c in range(columns):
            w[c, y + 2, pl.ds(ZP, nz)] = psi[y] * trial[c, y]

    def along(f):
        pair = f + pltpu.roll(f, 2, 1)
        return pltpu.roll(pair, 127, 1), pair + pltpu.roll(pair, 126, 1)

    def halo_stage(source, target, shift, weight):
        @pl.loop(0, half)
        def _(y):
            for z in range(0, nz, CHUNK):
                at = ZP + z
                f = source[0, y + 2, pl.ds(at, CHUNK)]
                near, far = neighbours(source, 0, y + 2, at, CHUNK)
                one, two = along(f)
                value = (far + two) - 16.0 * (near + one) + (scaled_halo[y, pl.ds(z, CHUNK)] - shift) * f
                if weight:
                    value = value - weight * w_halo[0, y + 2, pl.ds(at, CHUNK)]
                target[0, y + 2, pl.ds(at, CHUNK)] = value

        wrap_halo(target, half, nz, full)

    def mend(source):
        inner = lane % 32

        @pl.loop(0, half)
        def _(y):
            for z in range(0, nz, CHUNK):
                f = source[0, y + 2, pl.ds(ZP + z, CHUNK)]
                gap = f - pltpu.roll(f, 112, 1)
                gap = jnp.where(between(inner, 4, 6), gap, jnp.where(between(inner, 6, 8), -gap, 0.0))
                far = jnp.where(inner < 6, pltpu.roll(gap, 126, 1), pltpu.roll(gap, 2, 1))
                near = jnp.where(inner == 5, pltpu.roll(gap, 127, 1), pltpu.roll(gap, 1, 1))
                both = far - jnp.where(between(inner, 5, 7), 16.0 * near, 0.0)
                for h in range(2):
                    for c in range(columns):
                        moved = pltpu.roll(both, (122 - 64 * h - 32 * c) % 128, 1)
                        ends[c, y + h * half, pl.ds(z, CHUNK)] = jnp.where((lane < 2) | (lane >= 126), moved, 0.0)

    def stage(source, shift, weight, store):
        @pl.loop(0, ny)
        def _(y):
            for z in range(0, nz, CHUNK):
                at = ZP + z
                diagonal = scaled[y, pl.ds(z, CHUNK)] - shift if shift else scaled[y, pl.ds(z, CHUNK)]
                for c in range(columns):
                    f = source[c, y + 2, pl.ds(at, CHUNK)]
                    near, far = neighbours(source, c, y + 2, at, CHUNK)
                    one, two = along(f)
                    value = (far + two) - 16.0 * (near + one) + diagonal * f + ends[c, y, pl.ds(z, CHUNK)]
                    if weight:
                        value = value - weight * w[c, y + 2, pl.ds(at, CHUNK)]
                    store(c, y, z, value)

    def into(target):
        def store(c, y, z, value):
            target[c, y + 2, pl.ds(ZP + z, CHUNK)] = value

        return store

    def finish(c, y, z, value):
        term = (FINAL * psi[y, pl.ds(z, CHUNK)]) * value
        if adds:
            term = term + total[c, y, pl.ds(z, CHUNK)]
        out[c, y, pl.ds(z, CHUNK)] = term

    halo_stage(w_halo, u_halo, ALPHA, None)
    halo_stage(u_halo, v_halo, 0.0, BETA)
    mend(w_halo)
    stage(w, ALPHA, None, into(u))
    mend(u_halo)
    stage(u, 0.0, BETA, into(v))
    mend(v_halo)
    stage(v, 0.0, GAMMA, finish)


def vmem(count):
    return [pl.BlockSpec(memory_space=pltpu.VMEM)] * count


def params(mib):
    return pltpu.CompilerParams(vmem_limit_bytes=mib << 20)


def f32(*shape):
    return jax.ShapeDtypeStruct(shape, jnp.float32)


def ring_of(n):
    return [*range(0, n, 2), *range(n - 1 - n % 2, 0, -2)]


def body(trial, orbitals, potential, owner):
    columns, ny, nz, nx = trial.shape
    n, parts = lax.axis_size("cols"), lax.axis_size("sec")
    rounds = owner.shape[0]
    rows = ny * nz // n
    sec_up = [(i, (i + 1) % parts) for i in range(parts)]
    sec_down = [(j, i) for i, j in sec_up]

    last, first = pl.pallas_call(
        pack_kernel,
        out_shape=[f32(columns + 1, nz, nx)] * 2,
        in_specs=vmem(2),
        out_specs=vmem(2),
        compiler_params=params(8),
        name="pack",
    )(trial, potential)
    left = lax.ppermute(last, "sec", sec_up)
    right = lax.ppermute(first, "sec", sec_down)

    mine = lax.all_to_all(orbitals.reshape(n, rows, nx), "cols", 0, 0)
    ring = ring_of(n)
    order = jnp.array(ring, jnp.int32)
    spot = jnp.array([ring.index(i) for i in range(n)], jnp.int32)[lax.axis_index("cols")]
    clockwise = [(ring[i], ring[(i + 1) % n]) for i in range(n)]
    counter = [(j, i) for i, j in clockwise]

    own = [lax.dynamic_index_in_dim(mine, owner[r], 0, False) for r in range(rounds)]
    ahead, behind = list(own), list(own)
    blocks = [[own[r]] for r in range(rounds)]
    places = [spot]
    for step in range(1, n // 2 + 1):
        for r in range(rounds):
            ahead[r] = lax.ppermute(ahead[r], "cols", clockwise)
            blocks[r].append(ahead[r])
            if 2 * step < n:
                behind[r] = lax.ppermute(behind[r], "cols", counter)
                blocks[r].append(behind[r])
        places.append((spot - step) % n)
        if 2 * step < n:
            places.append((spot + step) % n)
    where = order[jnp.stack(places)]

    trial_halo, scaled, scaled_halo = pl.pallas_call(
        prepare_kernel,
        out_shape=[f32(ny // 2, nz, nx), f32(ny, nz, nx), f32(ny // 2, nz, nx)],
        in_specs=vmem(4),
        out_specs=vmem(3),
        compiler_params=params(10),
        name="prepare",
    )(trial, potential, left, right)

    total = None
    sections = []
    for r in range(rounds):
        psi, psi_last, psi_first = pl.pallas_call(
            functools.partial(gather_kernel, n, rows),
            out_shape=[f32(ny * nz, nx), f32(nz, nx), f32(nz, nx)],
            in_specs=[pl.BlockSpec(memory_space=pltpu.SMEM)] + vmem(n),
            out_specs=vmem(3),
            compiler_params=params(6),
            name="gather",
        )(where, *blocks[r])
        psi_left = lax.ppermute(psi_last, "sec", sec_up)
        psi_right = lax.ppermute(psi_first, "sec", sec_down)
        sections.append((psi.reshape(ny, nz, nx), psi_left, psi_right))
    for r in range(rounds):
        given = [*sections[r], trial, trial_halo, scaled, scaled_halo] + ([total] if r else [])
        planes = [pltpu.VMEM((columns, ny + 4, nz + 2 * ZP, nx), jnp.float32)] * 3
        planes.append(pltpu.VMEM((columns, ny, nz, nx), jnp.float32))
        halos = [pltpu.VMEM((1, ny // 2 + 4, nz + 2 * ZP, nx), jnp.float32)] * 3
        total = pl.pallas_call(
            functools.partial(round_kernel, r > 0),
            out_shape=f32(columns, ny, nz, nx),
            in_specs=vmem(len(given)),
            out_specs=pl.BlockSpec(memory_space=pltpu.VMEM),
            scratch_shapes=planes + halos,
            compiler_params=params(24),
            name="round",
        )(*given)
    return total


def solution(mesh):
    placed = (P("cols", None, None, "sec"), P("cols", None, None, "sec"), P(None, None, "sec"), P())
    return jax.shard_map(
        body, mesh=mesh, in_specs=placed, out_specs=P("cols", None, None, "sec"), check_vma=False
    )
```

```python
import functools

import jax
import jax.numpy as jnp
import numpy as np
from jax import lax
from jax.experimental import pallas as pl
from jax.experimental.pallas import tpu as pltpu
from jax.sharding import PartitionSpec as P

SCALE = 120.0
ALPHA = 0.6 * SCALE
BETA = 0.25 * SCALE**2
GAMMA = 0.1 * SCALE**3
FINAL = -2.0 / SCALE**3
HALO = 6
ZP = 8
CHUNK = 32


def lanes(rows):
    return lax.broadcasted_iota(jnp.int32, (rows, 128), 1)


def between(lane, low, high):
    return (lane >= low) & (lane < high)


def pack_edges(plane, ny, lane, first):
    tile = jnp.zeros_like(plane(0))
    for y in range(ny):
        source = 0 if first else 128 - HALO
        moved = pltpu.roll(plane(y), (8 * y - source) % 128, 1)
        tile = jnp.where(between(lane, 8 * y, 8 * y + HALO), moved, tile)
    return tile


def halo_plane(left, right, low, high, lane, y):
    inner = lane % 64
    tile = jnp.where(inner < 6, pltpu.roll(left, (-8 * y) % 128, 1), 0.0)
    tile = jnp.where(between(inner, 22, 28), pltpu.roll(right, (22 - 8 * y) % 128, 1), tile)
    tile = jnp.where(between(lane, 6, 12), pltpu.roll(low, 6, 1), tile)
    tile = jnp.where(between(lane, 16, 22), pltpu.roll(low, 22, 1), tile)
    tile = jnp.where(between(lane, 70, 76), pltpu.roll(high, 70, 1), tile)
    tile = jnp.where(between(lane, 80, 86), pltpu.roll(high, 86, 1), tile)
    return tile


def pack_kernel(trial, potential, last, first):
    columns, ny, nz, _ = trial.shape
    lane = lanes(nz)
    for out, leading in ((last, False), (first, True)):
        for c in range(columns):
            out[c] = pack_edges(lambda y: trial[c, y], ny, lane, leading)
        out[columns] = pack_edges(lambda y: potential[y], ny, lane, leading)


def prepare_kernel(trial, potential, left, right, trial_halo, scaled, scaled_halo):
    columns, ny, nz, _ = trial.shape
    lane = lanes(nz)
    half = ny // 2
    for y in range(half):
        tile = jnp.zeros((nz, 128), jnp.float32)
        for c in range(columns):
            part = halo_plane(left[c], right[c], trial[c, y], trial[c, y + half], lane, y)
            tile = tile + (pltpu.roll(part, 32 * c, 1) if c else part)
        trial_halo[y] = tile
        part = halo_plane(left[columns], right[columns], potential[y], potential[y + half], lane, y)
        scaled_halo[y] = 6.0 * (part + pltpu.roll(part, 32, 1)) - 6.0
    for y in range(ny):
        scaled[y] = 6.0 * potential[y] - 6.0


def gather_kernel(count, rows, where, *refs):
    blocks, (whole, last, first) = refs[:count], refs[count:]
    nz = last.shape[0]
    ny = whole.shape[0] // nz
    for k in range(count):
        whole[pl.ds(pl.multiple_of(where[k] * rows, 8), rows), :] = blocks[k][...]
    lane = lanes(nz)
    last[...] = pack_edges(lambda y: whole[y * nz : (y + 1) * nz], ny, lane, False)
    first[...] = pack_edges(lambda y: whole[y * nz : (y + 1) * nz], ny, lane, True)


def clear_borders(ref, ny, nz):
    for c in range(ref.shape[0]):
        for y in (0, 1, ny + 2, ny + 3):
            ref[c, y] = jnp.zeros_like(ref[c, y])

        @pl.loop(2, ny + 2)
        def _(y):
            ref[c, y, 0:ZP] = jnp.zeros((ZP, 128), jnp.float32)
            ref[c, y, ZP + nz : 2 * ZP + nz] = jnp.zeros((ZP, 128), jnp.float32)


def neighbours(ref, c, y, at, rows):
    near = (ref[c, y - 1, pl.ds(at, rows)] + ref[c, y + 1, pl.ds(at, rows)]) + (
        ref[c, y, pl.ds(at - 1, rows)] + ref[c, y, pl.ds(at + 1, rows)]
    )
    far = (ref[c, y - 2, pl.ds(at, rows)] + ref[c, y + 2, pl.ds(at, rows)]) + (
        ref[c, y, pl.ds(at - 2, rows)] + ref[c, y, pl.ds(at + 2, rows)]
    )
    return near, far


def wrap_halo(ref, half, nz, lane):
    inside = pl.ds(ZP, nz)
    for k in range(2):
        ref[0, half + 2 + k, inside] = jnp.where(lane < 64, pltpu.roll(ref[0, 2 + k, inside], 64, 1), 0.0)
        ref[0, k, inside] = jnp.where(lane >= 64, pltpu.roll(ref[0, half + k, inside], 64, 1), 0.0)


def bands():
    def weight(distance):
        return {1: -16.0, 2: 1.0}.get(abs(distance), 0.0)

    block = np.array([[weight(i - j) for j in range(128)] for i in range(128)], np.float32)
    sections = np.zeros((2, 6, 128, 2, 128), np.float32)
    for h in range(2):
        for c in range(2):
            ends = np.zeros((128, 128), np.float32)
            for i in range(HALO):
                for j in range(128):
                    ends[64 * h + 32 * c + i, j] = weight(i - HALO - j)
                    ends[64 * h + 32 * c + 16 + HALO + i, j] = weight(128 + i - j)
            for piece in range(2):
                sections[h, 2 * piece + c, :, c] = block
                sections[h, 4 + piece, :, c] = ends
    halo = np.zeros((2, 128, 128), np.float32)
    for start in range(0, 128, 16):
        halo[:, start : start + 2 * HALO, start : start + 2 * HALO] = block[: 2 * HALO, : 2 * HALO]
    return jnp.asarray(sections.reshape(2, 768, 256), jnp.bfloat16), jnp.asarray(halo.reshape(256, 128), jnp.bfloat16)


def round_scratch(columns, ny, nz, nx):
    half = ny // 2
    return (
        [pltpu.VMEM((columns, ny + 4, nz + 2 * ZP, nx), jnp.float32)] * 3
        + [pltpu.VMEM((1, half + 4, nz + 2 * ZP, nx), jnp.float32)] * 3
        + [
            pltpu.VMEM((ny * nz, 6 * nx), jnp.bfloat16),
            pltpu.VMEM((ny * nz, 2 * nx), jnp.float32),
            pltpu.VMEM((half * nz, nx), jnp.float32),
        ]
    )


def round_kernel(adds, psi, left, right, trial, trial_halo, scaled, scaled_halo, bands, halo_bands, *refs):
    if adds:
        total, *refs = refs
    out, w, u, v, w_halo, u_halo, v_halo, pieces, sums, halo_sums = refs
    columns, ny, nz, _ = trial.shape
    half = ny // 2
    full = lanes(nz)
    for ref in (w, u, v):
        clear_borders(ref, ny, nz)
    for ref in (w_halo, u_halo, v_halo):
        clear_borders(ref, half, nz)

    def split(value, row, first, second):
        high = value.astype(jnp.bfloat16)
        pieces[pl.ds(row, CHUNK), 128 * first : 128 * (first + 1)] = high
        rest = (value - high.astype(jnp.float32)).astype(jnp.bfloat16)
        pieces[pl.ds(row, CHUNK), 128 * second : 128 * (second + 1)] = rest

    def row_of(y, z):
        return pl.multiple_of(y * nz + z, CHUNK)

    def put(target, c, y, z, value):
        target[c, y + 2, pl.ds(ZP + z, CHUNK)] = value
        split(value, row_of(y, z), c, 2 + c)

    def put_halo(target, y, z, value):
        target[0, y + 2, pl.ds(ZP + z, CHUNK)] = value
        for h in range(2):
            split(value, row_of(y + h * half, z), 4, 5)

    for y in range(half):
        part = halo_plane(left[...], right[...], psi[y], psi[y + half], full, y)
        w_halo[0, y + 2, pl.ds(ZP, nz)] = (part + pltpu.roll(part, 32, 1)) * trial_halo[y]
    wrap_halo(w_halo, half, nz, full)

    @pl.loop(0, half)
    def _(y):
        for z in range(0, nz, CHUNK):
            put_halo(w_halo, y, z, w_halo[0, y + 2, pl.ds(ZP + z, CHUNK)])

    @pl.loop(0, ny)
    def _(y):
        for z in range(0, nz, CHUNK):
            here = psi[y, pl.ds(z, CHUNK)]
            for c in range(columns):
                put(w, c, y, z, here * trial[c, y, pl.ds(z, CHUNK)])

    def multiply():
        for h in range(2):
            rows = pl.ds(h * half * nz, half * nz)
            sums[rows, :] = jnp.dot(pieces[rows, :], bands[h], preferred_element_type=jnp.float32)

    def halo_stage(source, target, shift, weight):
        halo_sums[...] = jnp.dot(pieces[: half * nz, 512:], halo_bands[...], preferred_element_type=jnp.float32)

        @pl.loop(0, half)
        def _(y):
            for z in range(0, nz, CHUNK):
                at = ZP + z
                f = source[0, y + 2, pl.ds(at, CHUNK)]
                near, far = neighbours(source, 0, y + 2, at, CHUNK)
                value = (far + halo_sums[pl.ds(row_of(y, z), CHUNK), :]) - 16.0 * near
                value = value + (scaled_halo[y, pl.ds(z, CHUNK)] - shift) * f
                if weight:
                    value = value - weight * w_halo[0, y + 2, pl.ds(at, CHUNK)]
                put_halo(target, y, z, value)

        wrap_halo(target, half, nz, full)

    def stage(source, shift, weight, store):
        @pl.loop(0, ny)
        def _(y):
            for z in range(0, nz, CHUNK):
                at = ZP + z
                diagonal = scaled[y, pl.ds(z, CHUNK)] - shift if shift else scaled[y, pl.ds(z, CHUNK)]
                for c in range(columns):
                    f = source[c, y + 2, pl.ds(at, CHUNK)]
                    near, far = neighbours(source, c, y + 2, at, CHUNK)
                    value = (far + sums[pl.ds(row_of(y, z), CHUNK), 128 * c : 128 * (c + 1)]) - 16.0 * near
                    value = value + diagonal * f
                    if weight:
                        value = value - weight * w[c, y + 2, pl.ds(at, CHUNK)]
                    store(c, y, z, value)

    def into(target):
        return lambda c, y, z, value: put(target, c, y, z, value)

    def finish(c, y, z, value):
        term = (FINAL * psi[y, pl.ds(z, CHUNK)]) * value
        if adds:
            term = term + total[c, y, pl.ds(z, CHUNK)]
        out[c, y, pl.ds(z, CHUNK)] = term

    multiply()
    halo_stage(w_halo, u_halo, ALPHA, None)
    stage(w, ALPHA, None, into(u))
    multiply()
    halo_stage(u_halo, v_halo, 0.0, BETA)
    stage(u, 0.0, BETA, into(v))
    multiply()
    stage(v, 0.0, GAMMA, finish)


def vmem(count):
    return [pl.BlockSpec(memory_space=pltpu.VMEM)] * count


def params(mib):
    return pltpu.CompilerParams(vmem_limit_bytes=mib << 20)


def f32(*shape):
    return jax.ShapeDtypeStruct(shape, jnp.float32)


def ring_of(n):
    return [*range(0, n, 2), *range(n - 1 - n % 2, 0, -2)]


def body(trial, orbitals, potential, owner):
    columns, ny, nz, nx = trial.shape
    n, parts = lax.axis_size("cols"), lax.axis_size("sec")
    rounds = owner.shape[0]
    rows = ny * nz // n
    sec_up = [(i, (i + 1) % parts) for i in range(parts)]
    sec_down = [(j, i) for i, j in sec_up]

    last, first = pl.pallas_call(
        pack_kernel,
        out_shape=[f32(columns + 1, nz, nx)] * 2,
        in_specs=vmem(2),
        out_specs=vmem(2),
        compiler_params=params(8),
        name="pack",
    )(trial, potential)
    left = lax.ppermute(last, "sec", sec_up)
    right = lax.ppermute(first, "sec", sec_down)

    mine = lax.all_to_all(orbitals.reshape(n, rows, nx), "cols", 0, 0)
    ring = ring_of(n)
    order = jnp.array(ring, jnp.int32)
    spot = jnp.array([ring.index(i) for i in range(n)], jnp.int32)[lax.axis_index("cols")]
    clockwise = [(ring[i], ring[(i + 1) % n]) for i in range(n)]
    counter = [(j, i) for i, j in clockwise]

    own = [lax.dynamic_index_in_dim(mine, owner[r], 0, False) for r in range(rounds)]
    ahead, behind = list(own), list(own)
    blocks = [[own[r]] for r in range(rounds)]
    places = [spot]
    for step in range(1, n // 2 + 1):
        for r in range(rounds):
            ahead[r] = lax.ppermute(ahead[r], "cols", clockwise)
            blocks[r].append(ahead[r])
            if 2 * step < n:
                behind[r] = lax.ppermute(behind[r], "cols", counter)
                blocks[r].append(behind[r])
        places.append((spot - step) % n)
        if 2 * step < n:
            places.append((spot + step) % n)
    where = order[jnp.stack(places)]

    trial_halo, scaled, scaled_halo = pl.pallas_call(
        prepare_kernel,
        out_shape=[f32(ny // 2, nz, nx), f32(ny, nz, nx), f32(ny // 2, nz, nx)],
        in_specs=vmem(4),
        out_specs=vmem(3),
        compiler_params=params(10),
        name="prepare",
    )(trial, potential, left, right)

    total = None
    sections = []
    for r in range(rounds):
        psi, psi_last, psi_first = pl.pallas_call(
            functools.partial(gather_kernel, n, rows),
            out_shape=[f32(ny * nz, nx), f32(nz, nx), f32(nz, nx)],
            in_specs=[pl.BlockSpec(memory_space=pltpu.SMEM)] + vmem(n),
            out_specs=vmem(3),
            compiler_params=params(6),
            name="gather",
        )(where, *blocks[r])
        psi_left = lax.ppermute(psi_last, "sec", sec_up)
        psi_right = lax.ppermute(psi_first, "sec", sec_down)
        sections.append((psi.reshape(ny, nz, nx), psi_left, psi_right))
    matrices = bands()
    for r in range(rounds):
        given = [*sections[r], trial, trial_halo, scaled, scaled_halo, *matrices] + ([total] if r else [])
        total = pl.pallas_call(
            functools.partial(round_kernel, r > 0),
            out_shape=f32(columns, ny, nz, nx),
            in_specs=vmem(len(given)),
            out_specs=pl.BlockSpec(memory_space=pltpu.VMEM),
            scratch_shapes=round_scratch(columns, ny, nz, nx),
            compiler_params=params(32),
            name="round",
        )(*given)
    return total


def solution(mesh):
    placed = (P("cols", None, None, "sec"), P("cols", None, None, "sec"), P(None, None, "sec"), P())
    return jax.shard_map(
        body, mesh=mesh, in_specs=placed, out_specs=P("cols", None, None, "sec"), check_vma=False
    )
```

```python
import functools

import jax
import jax.numpy as jnp
import numpy as np
from jax import lax
from jax.experimental import pallas as pl
from jax.experimental.pallas import tpu as pltpu
from jax.sharding import PartitionSpec as P

SCALE = 120.0
ALPHA = 0.6 * SCALE
BETA = 0.25 * SCALE**2
GAMMA = 0.1 * SCALE**3
FINAL = -2.0 / SCALE**3
HALO = 6
ZP = 8
CHUNK = 32


def lanes(rows):
    return lax.broadcasted_iota(jnp.int32, (rows, 128), 1)


def between(lane, low, high):
    return (lane >= low) & (lane < high)


def pack_edges(plane, ny, lane, first):
    tile = jnp.zeros_like(plane(0))
    for y in range(ny):
        source = 0 if first else 128 - HALO
        moved = pltpu.roll(plane(y), (8 * y - source) % 128, 1)
        tile = jnp.where(between(lane, 8 * y, 8 * y + HALO), moved, tile)
    return tile


def halo_plane(left, right, low, high, lane, y):
    inner = lane % 64
    tile = jnp.where(inner < 6, pltpu.roll(left, (-8 * y) % 128, 1), 0.0)
    tile = jnp.where(between(inner, 22, 28), pltpu.roll(right, (22 - 8 * y) % 128, 1), tile)
    tile = jnp.where(between(lane, 6, 12), pltpu.roll(low, 6, 1), tile)
    tile = jnp.where(between(lane, 16, 22), pltpu.roll(low, 22, 1), tile)
    tile = jnp.where(between(lane, 70, 76), pltpu.roll(high, 70, 1), tile)
    tile = jnp.where(between(lane, 80, 86), pltpu.roll(high, 86, 1), tile)
    return tile


def pack_kernel(trial, potential, last, first):
    columns, ny, nz, _ = trial.shape
    lane = lanes(nz)
    for out, leading in ((last, False), (first, True)):
        for c in range(columns):
            out[c] = pack_edges(lambda y: trial[c, y], ny, lane, leading)
        out[columns] = pack_edges(lambda y: potential[y], ny, lane, leading)


def prepare_kernel(trial, potential, left, right, trial_halo, scaled, scaled_halo):
    columns, ny, nz, _ = trial.shape
    lane = lanes(nz)
    half = ny // 2
    for y in range(half):
        tile = jnp.zeros((nz, 128), jnp.float32)
        for c in range(columns):
            part = halo_plane(left[c], right[c], trial[c, y], trial[c, y + half], lane, y)
            tile = tile + (pltpu.roll(part, 32 * c, 1) if c else part)
        trial_halo[y] = tile
        part = halo_plane(left[columns], right[columns], potential[y], potential[y + half], lane, y)
        scaled_halo[y] = 6.0 * (part + pltpu.roll(part, 32, 1)) - 6.0
    for y in range(ny):
        scaled[y] = 6.0 * potential[y] - 6.0


def ring_of(n):
    return [*range(0, n, 2), *range(n - 1 - n % 2, 0, -2)]


def gather_kernel(n, rounds, *refs):
    blocks, (whole, last, first) = refs[:-3], refs[-3:]
    nz = last.shape[1]
    ny = whole.shape[1] // nz
    evens = (n + 1) // 2
    me = lax.axis_index("cols")
    spot = jnp.where(me % 2 == 0, me // 2, n - 1 - me // 2)
    rows = blocks[0].shape[1]

    def place(shift):
        position = lax.rem(spot + shift + n, n)
        device = jnp.where(position < evens, 2 * position, 2 * (n - 1 - position) + 1)
        return device * rows

    def put(block, start):
        size = block.shape[1]
        for r in range(rounds):
            whole[r, pl.ds(pl.multiple_of(start, 8), size), :] = block[r]

    put(blocks[0], place(0))
    for k, block in enumerate(blocks[1:]):
        step, ahead = k // 2 + 1, k % 2 == 0
        start = place(-step if ahead else step)
        put(block, start if ahead or block.shape[1] == rows else start + rows - block.shape[1])
    lane = lanes(nz)
    for r in range(rounds):
        last[r] = pack_edges(lambda y: whole[r, y * nz : (y + 1) * nz], ny, lane, False)
        first[r] = pack_edges(lambda y: whole[r, y * nz : (y + 1) * nz], ny, lane, True)


def clear_borders(ref, ny, nz):
    for c in range(ref.shape[0]):
        for y in (0, 1, ny + 2, ny + 3):
            ref[c, y] = jnp.zeros_like(ref[c, y])

        @pl.loop(2, ny + 2)
        def _(y):
            ref[c, y, 0:ZP] = jnp.zeros((ZP, 128), jnp.float32)
            ref[c, y, ZP + nz : 2 * ZP + nz] = jnp.zeros((ZP, 128), jnp.float32)


def neighbours(ref, c, y, at, rows):
    near = (ref[c, y - 1, pl.ds(at, rows)] + ref[c, y + 1, pl.ds(at, rows)]) + (
        ref[c, y, pl.ds(at - 1, rows)] + ref[c, y, pl.ds(at + 1, rows)]
    )
    far = (ref[c, y - 2, pl.ds(at, rows)] + ref[c, y + 2, pl.ds(at, rows)]) + (
        ref[c, y, pl.ds(at - 2, rows)] + ref[c, y, pl.ds(at + 2, rows)]
    )
    return near, far


def wrap_halo(ref, half, nz, lane):
    inside = pl.ds(ZP, nz)
    for k in range(2):
        ref[0, half + 2 + k, inside] = jnp.where(lane < 64, pltpu.roll(ref[0, 2 + k, inside], 64, 1), 0.0)
        ref[0, k, inside] = jnp.where(lane >= 64, pltpu.roll(ref[0, half + k, inside], 64, 1), 0.0)


def bands():
    def weight(distance):
        return {1: -16.0, 2: 1.0}.get(abs(distance), 0.0)

    block = np.array([[weight(i - j) for j in range(128)] for i in range(128)], np.float32)
    sections = np.zeros((2, 6, 128, 2, 128), np.float32)
    for h in range(2):
        for c in range(2):
            ends = np.zeros((128, 128), np.float32)
            for i in range(HALO):
                for j in range(128):
                    ends[64 * h + 32 * c + i, j] = weight(i - HALO - j)
                    ends[64 * h + 32 * c + 16 + HALO + i, j] = weight(128 + i - j)
            for piece in range(2):
                sections[h, 2 * piece + c, :, c] = block
                sections[h, 4 + piece, :, c] = ends
    halo = np.zeros((2, 128, 128), np.float32)
    for start in range(0, 128, 16):
        halo[:, start : start + 2 * HALO, start : start + 2 * HALO] = block[: 2 * HALO, : 2 * HALO]
    return jnp.asarray(sections.reshape(2, 768, 256), jnp.bfloat16), jnp.asarray(halo.reshape(256, 128), jnp.bfloat16)


def round_scratch(columns, ny, nz, nx):
    half = ny // 2
    return (
        [pltpu.VMEM((columns, ny + 4, nz + 2 * ZP, nx), jnp.float32)] * 3
        + [pltpu.VMEM((1, half + 4, nz + 2 * ZP, nx), jnp.float32)] * 3
        + [
            pltpu.VMEM((ny * nz, 6 * nx), jnp.bfloat16),
            pltpu.VMEM((ny * nz, 2 * nx), jnp.float32),
            pltpu.VMEM((half * nz, nx), jnp.float32),
        ]
    )


def round_kernel(turn, psi, left, right, trial, trial_halo, scaled, scaled_halo, bands, halo_bands, *refs):
    psi, left, right = psi.at[turn], left.at[turn], right.at[turn]
    if turn:
        total, *refs = refs
    out, w, u, v, w_halo, u_halo, v_halo, pieces, sums, halo_sums = refs
    columns, ny, nz, _ = trial.shape
    half = ny // 2
    full = lanes(nz)
    for ref in (w, u, v):
        clear_borders(ref, ny, nz)
    for ref in (w_halo, u_halo, v_halo):
        clear_borders(ref, half, nz)

    def split(value, row, first, second):
        high = value.astype(jnp.bfloat16)
        pieces[pl.ds(row, CHUNK), 128 * first : 128 * (first + 1)] = high
        rest = (value - high.astype(jnp.float32)).astype(jnp.bfloat16)
        pieces[pl.ds(row, CHUNK), 128 * second : 128 * (second + 1)] = rest

    def row_of(y, z):
        return pl.multiple_of(y * nz + z, CHUNK)

    def put(target, c, y, z, value):
        target[c, y + 2, pl.ds(ZP + z, CHUNK)] = value
        split(value, row_of(y, z), c, 2 + c)

    def put_halo(target, y, z, value):
        target[0, y + 2, pl.ds(ZP + z, CHUNK)] = value
        for h in range(2):
            split(value, row_of(y + h * half, z), 4, 5)

    for y in range(half):
        part = halo_plane(left[...], right[...], psi[y], psi[y + half], full, y)
        w_halo[0, y + 2, pl.ds(ZP, nz)] = (part + pltpu.roll(part, 32, 1)) * trial_halo[y]
    wrap_halo(w_halo, half, nz, full)

    @pl.loop(0, half)
    def _(y):
        for z in range(0, nz, CHUNK):
            put_halo(w_halo, y, z, w_halo[0, y + 2, pl.ds(ZP + z, CHUNK)])

    @pl.loop(0, ny)
    def _(y):
        for z in range(0, nz, CHUNK):
            here = psi[y, pl.ds(z, CHUNK)]
            for c in range(columns):
                put(w, c, y, z, here * trial[c, y, pl.ds(z, CHUNK)])

    def multiply():
        for h in range(2):
            rows = pl.ds(h * half * nz, half * nz)
            sums[rows, :] = jnp.dot(pieces[rows, :], bands[h], preferred_element_type=jnp.float32)

    def halo_stage(source, target, shift, weight):
        halo_sums[...] = jnp.dot(pieces[: half * nz, 512:], halo_bands[...], preferred_element_type=jnp.float32)

        @pl.loop(0, half)
        def _(y):
            for z in range(0, nz, CHUNK):
                at = ZP + z
                f = source[0, y + 2, pl.ds(at, CHUNK)]
                near, far = neighbours(source, 0, y + 2, at, CHUNK)
                value = (far + halo_sums[pl.ds(row_of(y, z), CHUNK), :]) - 16.0 * near
                value = value + (scaled_halo[y, pl.ds(z, CHUNK)] - shift) * f
                if weight:
                    value = value - weight * w_halo[0, y + 2, pl.ds(at, CHUNK)]
                put_halo(target, y, z, value)

        wrap_halo(target, half, nz, full)

    def stage(source, shift, weight, store):
        @pl.loop(0, ny)
        def _(y):
            for z in range(0, nz, CHUNK):
                at = ZP + z
                diagonal = scaled[y, pl.ds(z, CHUNK)] - shift if shift else scaled[y, pl.ds(z, CHUNK)]
                for c in range(columns):
                    f = source[c, y + 2, pl.ds(at, CHUNK)]
                    near, far = neighbours(source, c, y + 2, at, CHUNK)
                    value = (far + sums[pl.ds(row_of(y, z), CHUNK), 128 * c : 128 * (c + 1)]) - 16.0 * near
                    value = value + diagonal * f
                    if weight:
                        value = value - weight * w[c, y + 2, pl.ds(at, CHUNK)]
                    store(c, y, z, value)

    def into(target):
        return lambda c, y, z, value: put(target, c, y, z, value)

    def finish(c, y, z, value):
        term = (FINAL * psi[y, pl.ds(z, CHUNK)]) * value
        if turn:
            term = term + total[c, y, pl.ds(z, CHUNK)]
        out[c, y, pl.ds(z, CHUNK)] = term

    multiply()
    halo_stage(w_halo, u_halo, ALPHA, None)
    stage(w, ALPHA, None, into(u))
    multiply()
    halo_stage(u_halo, v_halo, 0.0, BETA)
    stage(u, 0.0, BETA, into(v))
    multiply()
    stage(v, 0.0, GAMMA, finish)


def vmem(count):
    return [pl.BlockSpec(memory_space=pltpu.VMEM)] * count


def params(mib):
    return pltpu.CompilerParams(vmem_limit_bytes=mib << 20)


def f32(*shape):
    return jax.ShapeDtypeStruct(shape, jnp.float32)


def body(trial, orbitals, potential, owner):
    columns, ny, nz, nx = trial.shape
    n, parts = lax.axis_size("cols"), lax.axis_size("sec")
    rounds = owner.shape[0]
    rows = ny * nz // n
    sec_up = [(i, (i + 1) % parts) for i in range(parts)]
    sec_down = [(j, i) for i, j in sec_up]

    last, first = pl.pallas_call(
        pack_kernel,
        out_shape=[f32(columns + 1, nz, nx)] * 2,
        in_specs=vmem(2),
        out_specs=vmem(2),
        compiler_params=params(8),
        name="pack",
    )(trial, potential)
    left = lax.ppermute(last, "sec", sec_up)
    right = lax.ppermute(first, "sec", sec_down)

    mine = lax.all_to_all(orbitals.reshape(n, rows, nx), "cols", 0, 0)
    prepared = pl.pallas_call(
        prepare_kernel,
        out_shape=[f32(ny // 2, nz, nx), f32(ny, nz, nx), f32(ny // 2, nz, nx)],
        in_specs=vmem(4),
        out_specs=vmem(3),
        compiler_params=params(10),
        name="prepare",
    )(trial, potential, left, right)
    mine, (trial_halo, scaled, scaled_halo) = lax.optimization_barrier((mine, prepared))

    ring = ring_of(n)
    clockwise = [(ring[i], ring[(i + 1) % n]) for i in range(n)]
    counter = [(j, i) for i, j in clockwise]
    own = jnp.concatenate([lax.dynamic_slice_in_dim(mine, owner[r], 1, 0) for r in range(rounds)])
    ahead = behind = own
    blocks = [own]
    for step in range(1, n // 2 + 1):
        if 2 * step == n:
            cut = rows // 16 * 8
            ahead, behind = ahead[:, :cut], behind[:, cut:]
        ahead = lax.ppermute(ahead, "cols", clockwise)
        behind = lax.ppermute(behind, "cols", counter)
        blocks += [ahead, behind]

    psi, psi_last, psi_first = pl.pallas_call(
        functools.partial(gather_kernel, n, rounds),
        out_shape=[f32(rounds, ny * nz, nx), f32(rounds, nz, nx), f32(rounds, nz, nx)],
        in_specs=vmem(len(blocks)),
        out_specs=vmem(3),
        compiler_params=params(10),
        name="gather",
    )(*blocks)
    psi = psi.reshape(rounds, ny, nz, nx)
    psi_left = lax.ppermute(psi_last, "sec", sec_up)
    psi_right = lax.ppermute(psi_first, "sec", sec_down)
    total = None
    matrices = bands()
    for r in range(rounds):
        given = [psi, psi_left, psi_right, trial, trial_halo, scaled, scaled_halo, *matrices] + ([total] if r else [])
        total = pl.pallas_call(
            functools.partial(round_kernel, r),
            out_shape=f32(columns, ny, nz, nx),
            in_specs=vmem(len(given)),
            out_specs=pl.BlockSpec(memory_space=pltpu.VMEM),
            scratch_shapes=round_scratch(columns, ny, nz, nx),
            compiler_params=params(32),
            name="round",
        )(*given)
    return total


def solution(mesh):
    placed = (P("cols", None, None, "sec"), P("cols", None, None, "sec"), P(None, None, "sec"), P())
    return jax.shard_map(
        body, mesh=mesh, in_specs=placed, out_specs=P("cols", None, None, "sec"), check_vma=False
    )
```

```python
import functools

import jax
import jax.numpy as jnp
import numpy as np
from jax import lax
from jax.experimental import pallas as pl
from jax.experimental.pallas import tpu as pltpu
from jax.sharding import PartitionSpec as P

SCALE = 120.0
ALPHA = 0.6 * SCALE
BETA = 0.25 * SCALE**2
GAMMA = 0.1 * SCALE**3
FINAL = -2.0 / SCALE**3
HALO = 6
ZP = 8
CHUNK = 32


def lanes(rows):
    return lax.broadcasted_iota(jnp.int32, (rows, 128), 1)


def between(lane, low, high):
    return (lane >= low) & (lane < high)


def pack_edges(plane, ny, lane, first):
    tile = jnp.zeros_like(plane(0))
    for y in range(ny):
        source = 0 if first else 128 - HALO
        moved = pltpu.roll(plane(y), (8 * y - source) % 128, 1)
        tile = jnp.where(between(lane, 8 * y, 8 * y + HALO), moved, tile)
    return tile


def halo_plane(left, right, low, high, lane, y):
    inner = lane % 64
    tile = jnp.where(inner < 6, pltpu.roll(left, (-8 * y) % 128, 1), 0.0)
    tile = jnp.where(between(inner, 22, 28), pltpu.roll(right, (22 - 8 * y) % 128, 1), tile)
    tile = jnp.where(between(lane, 6, 12), pltpu.roll(low, 6, 1), tile)
    tile = jnp.where(between(lane, 16, 22), pltpu.roll(low, 22, 1), tile)
    tile = jnp.where(between(lane, 70, 76), pltpu.roll(high, 70, 1), tile)
    tile = jnp.where(between(lane, 80, 86), pltpu.roll(high, 86, 1), tile)
    return tile


def pack_kernel(trial, potential, last, first):
    columns, ny, nz, _ = trial.shape
    lane = lanes(nz)
    for out, leading in ((last, False), (first, True)):
        for c in range(columns):
            out[c] = pack_edges(lambda y: trial[c, y], ny, lane, leading)
        out[columns] = pack_edges(lambda y: potential[y], ny, lane, leading)


def prepare_kernel(trial, potential, left, right, trial_halo, scaled, scaled_halo):
    columns, ny, nz, _ = trial.shape
    lane = lanes(nz)
    half = ny // 2
    for y in range(half):
        tile = jnp.zeros((nz, 128), jnp.float32)
        for c in range(columns):
            part = halo_plane(left[c], right[c], trial[c, y], trial[c, y + half], lane, y)
            tile = tile + (pltpu.roll(part, 32 * c, 1) if c else part)
        trial_halo[y] = tile
        part = halo_plane(left[columns], right[columns], potential[y], potential[y + half], lane, y)
        scaled_halo[y] = 6.0 * (part + pltpu.roll(part, 32, 1)) - 6.0
    for y in range(ny):
        scaled[y] = 6.0 * potential[y] - 6.0


def ring_of(n):
    return [*range(0, n, 2), *range(n - 1 - n % 2, 0, -2)]


def gather_kernel(n, rounds, owner, *refs):
    blocks, (whole, last, first) = refs[:-3], refs[-3:]
    nz = last.shape[1]
    ny = whole.shape[1] // nz
    evens = (n + 1) // 2
    me = lax.axis_index("cols")
    spot = jnp.where(me % 2 == 0, me // 2, n - 1 - me // 2)
    rows = blocks[0].shape[1]

    def put(block, shift, last_part):
        position = lax.rem(spot + shift + n, n)
        device = jnp.where(position < evens, 2 * position, 2 * (n - 1 - position) + 1)
        size = block.shape[1]
        for r in range(rounds):
            start = (device ^ owner[r]) * rows + (rows - size if last_part else 0)
            whole[r, pl.ds(pl.multiple_of(start, 8), size), :] = block[r]

    put(blocks[0], 0, False)
    for k, block in enumerate(blocks[1:]):
        step, ahead = k // 2 + 1, k % 2 == 0
        put(block, -step if ahead else step, not ahead)
    lane = lanes(nz)
    for r in range(rounds):
        last[r] = pack_edges(lambda y: whole[r, y * nz : (y + 1) * nz], ny, lane, False)
        first[r] = pack_edges(lambda y: whole[r, y * nz : (y + 1) * nz], ny, lane, True)


def clear_borders(ref, ny, nz):
    for c in range(ref.shape[0]):
        for y in (0, 1, ny + 2, ny + 3):
            ref[c, y] = jnp.zeros_like(ref[c, y])

        @pl.loop(2, ny + 2)
        def _(y):
            ref[c, y, 0:ZP] = jnp.zeros((ZP, 128), jnp.float32)
            ref[c, y, ZP + nz : 2 * ZP + nz] = jnp.zeros((ZP, 128), jnp.float32)


def neighbours(ref, c, y, at, rows):
    near = (ref[c, y - 1, pl.ds(at, rows)] + ref[c, y + 1, pl.ds(at, rows)]) + (
        ref[c, y, pl.ds(at - 1, rows)] + ref[c, y, pl.ds(at + 1, rows)]
    )
    far = (ref[c, y - 2, pl.ds(at, rows)] + ref[c, y + 2, pl.ds(at, rows)]) + (
        ref[c, y, pl.ds(at - 2, rows)] + ref[c, y, pl.ds(at + 2, rows)]
    )
    return near, far


def wrap_halo(ref, half, nz, lane):
    inside = pl.ds(ZP, nz)
    for k in range(2):
        ref[0, half + 2 + k, inside] = jnp.where(lane < 64, pltpu.roll(ref[0, 2 + k, inside], 64, 1), 0.0)
        ref[0, k, inside] = jnp.where(lane >= 64, pltpu.roll(ref[0, half + k, inside], 64, 1), 0.0)


def bands():
    def weight(distance):
        return {1: -16.0, 2: 1.0}.get(abs(distance), 0.0)

    block = np.array([[weight(i - j) for j in range(128)] for i in range(128)], np.float32)
    sections = np.zeros((2, 6, 128, 2, 128), np.float32)
    for h in range(2):
        for c in range(2):
            ends = np.zeros((128, 128), np.float32)
            for i in range(HALO):
                for j in range(128):
                    ends[64 * h + 32 * c + i, j] = weight(i - HALO - j)
                    ends[64 * h + 32 * c + 16 + HALO + i, j] = weight(128 + i - j)
            for piece in range(2):
                sections[h, 2 * piece + c, :, c] = block
                sections[h, 4 + piece, :, c] = ends
    halo = np.zeros((2, 128, 128), np.float32)
    for start in range(0, 128, 16):
        halo[:, start : start + 2 * HALO, start : start + 2 * HALO] = block[: 2 * HALO, : 2 * HALO]
    return jnp.asarray(sections.reshape(2, 768, 256), jnp.bfloat16), jnp.asarray(halo.reshape(256, 128), jnp.bfloat16)


def round_scratch(columns, ny, nz, nx):
    half = ny // 2
    return (
        [pltpu.VMEM((columns, ny + 4, nz + 2 * ZP, nx), jnp.float32)] * 3
        + [pltpu.VMEM((1, half + 4, nz + 2 * ZP, nx), jnp.float32)] * 3
        + [
            pltpu.VMEM((ny * nz, 6 * nx), jnp.bfloat16),
            pltpu.VMEM((ny * nz, 2 * nx), jnp.float32),
            pltpu.VMEM((half * nz, nx), jnp.float32),
        ]
    )


def round_kernel(turn, psi, left, right, trial, trial_halo, scaled, scaled_halo, bands, halo_bands, *refs):
    psi, left, right = psi.at[turn], left.at[turn], right.at[turn]
    if turn:
        total, *refs = refs
    out, w, u, v, w_halo, u_halo, v_halo, pieces, sums, halo_sums = refs
    columns, ny, nz, _ = trial.shape
    half = ny // 2
    full = lanes(nz)
    for ref in (w, u, v):
        clear_borders(ref, ny, nz)
    for ref in (w_halo, u_halo, v_halo):
        clear_borders(ref, half, nz)

    def split(value, row, first, second):
        high = value.astype(jnp.bfloat16)
        pieces[pl.ds(row, CHUNK), 128 * first : 128 * (first + 1)] = high
        rest = (value - high.astype(jnp.float32)).astype(jnp.bfloat16)
        pieces[pl.ds(row, CHUNK), 128 * second : 128 * (second + 1)] = rest

    def row_of(y, z):
        return pl.multiple_of(y * nz + z, CHUNK)

    def put(target, c, y, z, value):
        target[c, y + 2, pl.ds(ZP + z, CHUNK)] = value
        split(value, row_of(y, z), c, 2 + c)

    def put_halo(target, y, z, value):
        target[0, y + 2, pl.ds(ZP + z, CHUNK)] = value
        for h in range(2):
            split(value, row_of(y + h * half, z), 4, 5)

    for y in range(half):
        part = halo_plane(left[...], right[...], psi[y], psi[y + half], full, y)
        w_halo[0, y + 2, pl.ds(ZP, nz)] = (part + pltpu.roll(part, 32, 1)) * trial_halo[y]
    wrap_halo(w_halo, half, nz, full)

    @pl.loop(0, half)
    def _(y):
        for z in range(0, nz, CHUNK):
            put_halo(w_halo, y, z, w_halo[0, y + 2, pl.ds(ZP + z, CHUNK)])

    @pl.loop(0, ny)
    def _(y):
        for z in range(0, nz, CHUNK):
            here = psi[y, pl.ds(z, CHUNK)]
            for c in range(columns):
                put(w, c, y, z, here * trial[c, y, pl.ds(z, CHUNK)])

    def multiply():
        for h in range(2):
            rows = pl.ds(h * half * nz, half * nz)
            sums[rows, :] = jnp.dot(pieces[rows, :], bands[h], preferred_element_type=jnp.float32)

    def halo_stage(source, target, shift, weight):
        halo_sums[...] = jnp.dot(pieces[: half * nz, 512:], halo_bands[...], preferred_element_type=jnp.float32)

        @pl.loop(0, half)
        def _(y):
            for z in range(0, nz, CHUNK):
                at = ZP + z
                f = source[0, y + 2, pl.ds(at, CHUNK)]
                near, far = neighbours(source, 0, y + 2, at, CHUNK)
                value = (far + halo_sums[pl.ds(row_of(y, z), CHUNK), :]) - 16.0 * near
                value = value + (scaled_halo[y, pl.ds(z, CHUNK)] - shift) * f
                if weight:
                    value = value - weight * w_halo[0, y + 2, pl.ds(at, CHUNK)]
                put_halo(target, y, z, value)

        wrap_halo(target, half, nz, full)

    def stage(source, shift, weight, store):
        @pl.loop(0, ny)
        def _(y):
            for z in range(0, nz, CHUNK):
                at = ZP + z
                diagonal = scaled[y, pl.ds(z, CHUNK)] - shift if shift else scaled[y, pl.ds(z, CHUNK)]
                for c in range(columns):
                    f = source[c, y + 2, pl.ds(at, CHUNK)]
                    near, far = neighbours(source, c, y + 2, at, CHUNK)
                    value = (far + sums[pl.ds(row_of(y, z), CHUNK), 128 * c : 128 * (c + 1)]) - 16.0 * near
                    value = value + diagonal * f
                    if weight:
                        value = value - weight * w[c, y + 2, pl.ds(at, CHUNK)]
                    store(c, y, z, value)

    def into(target):
        return lambda c, y, z, value: put(target, c, y, z, value)

    def finish(c, y, z, value):
        term = (FINAL * psi[y, pl.ds(z, CHUNK)]) * value
        if turn:
            term = term + total[c, y, pl.ds(z, CHUNK)]
        out[c, y, pl.ds(z, CHUNK)] = term

    multiply()
    halo_stage(w_halo, u_halo, ALPHA, None)
    stage(w, ALPHA, None, into(u))
    multiply()
    halo_stage(u_halo, v_halo, 0.0, BETA)
    stage(u, 0.0, BETA, into(v))
    multiply()
    stage(v, 0.0, GAMMA, finish)


def vmem(count):
    return [pl.BlockSpec(memory_space=pltpu.VMEM)] * count


def params(mib):
    return pltpu.CompilerParams(vmem_limit_bytes=mib << 20)


def f32(*shape):
    return jax.ShapeDtypeStruct(shape, jnp.float32)


def exchange(pieces):
    n = pieces.shape[0]
    if n > 16:
        arranged = jnp.take(pieces, lax.axis_index("cols") ^ jnp.arange(n), axis=0)
        got = lax.all_to_all(arranged, "cols", 0, 0)
        return [got[s : s + 1] for s in range(n)]
    got = {0: pieces[:1]}
    reach = 1 << (n - 1).bit_length() - 1
    for group in ([k for k in range(reach, n)], [k for k in range(1, reach)]):
        sent = [pieces[k : k + 1] for k in group]
        pieces, *sent = lax.optimization_barrier([pieces, *sent])
        for k, piece in sorted(zip(group, sent), key=lambda pair: (-pair[0].bit_length(), pair[0] & 1, pair[0])):
            got[k] = lax.ppermute(piece, "cols", [(i, i ^ k) for i in range(n)])
    return [got[k] for k in range(n)]


def pick_kernel(owner, *refs):
    got, own = refs[:-1], refs[-1]
    me = lax.axis_index("cols") if len(got) <= 16 else 0
    for r in range(own.shape[0]):
        for k, piece in enumerate(got):

            @pl.when((me ^ owner[r]) == k)
            def _():
                own[r] = piece[0]


def cost(mib):
    return pl.CostEstimate(flops=0, transcendentals=0, bytes_accessed=mib << 20)


def body(trial, orbitals, potential, owner):
    columns, ny, nz, nx = trial.shape
    n, parts = lax.axis_size("cols"), lax.axis_size("sec")
    rounds = owner.shape[0]
    rows = ny * nz // n
    sec_up = [(i, (i + 1) % parts) for i in range(parts)]
    sec_down = [(j, i) for i, j in sec_up]

    got = exchange(orbitals.reshape(n, rows, nx))
    last, first = pl.pallas_call(
        pack_kernel,
        out_shape=[f32(columns + 1, nz, nx)] * 2,
        in_specs=vmem(2),
        out_specs=vmem(2),
        compiler_params=params(8),
        cost_estimate=cost(6),
    )(trial, potential)
    left = lax.ppermute(last, "sec", sec_up)
    right = lax.ppermute(first, "sec", sec_down)
    prepared = pl.pallas_call(
        prepare_kernel,
        out_shape=[f32(ny // 2, nz, nx), f32(ny, nz, nx), f32(ny // 2, nz, nx)],
        in_specs=vmem(4),
        out_specs=vmem(3),
        compiler_params=params(10),
        cost_estimate=cost(10),
    )(trial, potential, left, right)
    trial_halo, scaled, scaled_halo = prepared

    ring = ring_of(n)
    clockwise = [(ring[i], ring[(i + 1) % n]) for i in range(n)]
    counter = [(j, i) for i, j in clockwise]
    smem = [pl.BlockSpec(memory_space=pltpu.SMEM)]
    own = pl.pallas_call(
        pick_kernel,
        out_shape=f32(rounds, rows, nx),
        in_specs=smem + vmem(n),
        out_specs=pl.BlockSpec(memory_space=pltpu.VMEM),
        compiler_params=params(4),
        name="pick",
    )(owner, *got)
    ahead = behind = own
    blocks = [own]
    for step in range(1, n // 2 + 1):
        if 2 * step == n:
            cut = rows // 16 * 8
            ahead, behind = ahead[:, :cut], behind[:, cut:]
        ahead = lax.ppermute(ahead, "cols", clockwise)
        behind = lax.ppermute(behind, "cols", counter)
        blocks += [ahead, behind]

    psi, psi_last, psi_first = pl.pallas_call(
        functools.partial(gather_kernel, n, rounds),
        out_shape=[f32(rounds, ny * nz, nx), f32(rounds, nz, nx), f32(rounds, nz, nx)],
        in_specs=smem + vmem(len(blocks)),
        out_specs=vmem(3),
        compiler_params=params(10),
        name="gather",
    )(owner, *blocks)
    psi = psi.reshape(rounds, ny, nz, nx)
    psi_left = lax.ppermute(psi_last, "sec", sec_up)
    psi_right = lax.ppermute(psi_first, "sec", sec_down)
    total = None
    matrices = bands()
    for r in range(rounds):
        given = [psi, psi_left, psi_right, trial, trial_halo, scaled, scaled_halo, *matrices] + ([total] if r else [])
        total = pl.pallas_call(
            functools.partial(round_kernel, r),
            out_shape=f32(columns, ny, nz, nx),
            in_specs=vmem(len(given)),
            out_specs=pl.BlockSpec(memory_space=pltpu.VMEM),
            scratch_shapes=round_scratch(columns, ny, nz, nx),
            compiler_params=params(32),
            name="round",
        )(*given)
    return total


def solution(mesh):
    placed = (P("cols", None, None, "sec"), P("cols", None, None, "sec"), P(None, None, "sec"), P())

    return jax.shard_map(body, mesh=mesh, in_specs=placed, out_specs=P("cols", None, None, "sec"), check_vma=False)
```

```python
import functools

import jax
import jax.numpy as jnp
import numpy as np
from jax import lax
from jax.experimental import pallas as pl
from jax.experimental.pallas import tpu as pltpu
from jax.sharding import PartitionSpec as P

SCALE = 120.0
ALPHA = 0.6 * SCALE
BETA = 0.25 * SCALE**2
GAMMA = 0.1 * SCALE**3
FINAL = -2.0 / SCALE**3
HALO = 6
ZP = 8
CHUNK = 32
SHORT = 16
DEPTH = 4


def lanes(rows):
    return lax.broadcasted_iota(jnp.int32, (rows, 128), 1)


def between(lane, low, high):
    return (lane >= low) & (lane < high)


def pack_edges(plane, ny, lane, first):
    tile = jnp.zeros_like(plane(0))
    for y in range(ny):
        source = 0 if first else 128 - HALO
        moved = pltpu.roll(plane(y), (8 * y - source) % 128, 1)
        tile = jnp.where(between(lane, 8 * y, 8 * y + HALO), moved, tile)
    return tile


def outer_lanes(left, right, lane, y):
    inner = lane % 64
    tile = jnp.where(inner < 6, pltpu.roll(left, (-8 * y) % 128, 1), 0.0)
    return jnp.where(between(inner, 22, 28), pltpu.roll(right, (22 - 8 * y) % 128, 1), tile)


def inner_lanes(low, high, lane):
    tile = jnp.where(between(lane, 6, 12), pltpu.roll(low, 6, 1), 0.0)
    tile = jnp.where(between(lane, 16, 22), pltpu.roll(low, 22, 1), tile)
    tile = jnp.where(between(lane, 70, 76), pltpu.roll(high, 70, 1), tile)
    return jnp.where(between(lane, 80, 86), pltpu.roll(high, 86, 1), tile)


def halo_plane(left, right, low, high, lane, y):
    return outer_lanes(left, right, lane, y) + inner_lanes(low, high, lane)


def pack_kernel(trial, potential, last, first):
    columns, ny, nz, _ = trial.shape
    lane = lanes(nz)
    for out, leading in ((last, False), (first, True)):
        for c in range(columns):
            out[c] = pack_edges(lambda y: trial[c, y], ny, lane, leading)
        out[columns] = pack_edges(lambda y: potential[y], ny, lane, leading)


def prepare_kernel(trial, potential, left, right, trial_halo, scaled, scaled_halo):
    columns, ny, nz, _ = trial.shape
    lane = lanes(nz)
    half = ny // 2
    for y in range(half):
        tile = jnp.zeros((nz, 128), jnp.float32)
        for c in range(columns):
            part = halo_plane(left[c], right[c], trial[c, y], trial[c, y + half], lane, y)
            tile = tile + (pltpu.roll(part, 32 * c, 1) if c else part)
        trial_halo[y] = tile
        part = halo_plane(left[columns], right[columns], potential[y], potential[y + half], lane, y)
        scaled_halo[y] = 6.0 * (part + pltpu.roll(part, 32, 1)) - 6.0
    for y in range(ny):
        scaled[y] = 6.0 * potential[y] - 6.0


def ring_of(n):
    return [*range(0, n, 2), *range(n - 1 - n % 2, 0, -2)]


def gather_kernel(n, rounds, owner, *refs):
    blocks, (whole, last, first) = refs[:-3], refs[-3:]
    nz = last.shape[1]
    ny = whole.shape[1] // nz
    evens = (n + 1) // 2
    me = lax.axis_index("cols")
    spot = jnp.where(me % 2 == 0, me // 2, n - 1 - me // 2)
    rows = blocks[0].shape[1]

    def put(block, shift, last_part):
        position = lax.rem(spot + shift + n, n)
        device = jnp.where(position < evens, 2 * position, 2 * (n - 1 - position) + 1)
        size = block.shape[1]
        for r in range(rounds):
            start = (device ^ owner[r]) * rows + (rows - size if last_part else 0)
            whole[r, pl.ds(pl.multiple_of(start, 8), size), :] = block[r]

    put(blocks[0], 0, False)
    for k, block in enumerate(blocks[1:]):
        step, ahead = k // 2 + 1, k % 2 == 0
        put(block, -step if ahead else step, not ahead)
    lane = lanes(nz)
    for r in range(rounds):
        last[r] = pack_edges(lambda y: whole[r, y * nz : (y + 1) * nz], ny, lane, False)
        first[r] = pack_edges(lambda y: whole[r, y * nz : (y + 1) * nz], ny, lane, True)


def clear_borders(ref, nz, planes):
    zero = jnp.zeros((ZP, 128), jnp.float32)
    for c in range(ref.shape[0]):
        for y in range(ref.shape[1]):
            if y in planes:
                ref[c, y] = jnp.zeros_like(ref[c, y])
            else:
                ref[c, y, 0:ZP] = zero
                ref[c, y, ZP + nz : 2 * ZP + nz] = zero


def rows_around(ref, c, y, at, rows):
    near = ref[c, y, pl.ds(at - 1, rows)] + ref[c, y, pl.ds(at + 1, rows)]
    far = ref[c, y, pl.ds(at - 2, rows)] + ref[c, y, pl.ds(at + 2, rows)]
    return near, far


def wrap_halo(ref, half, nz, lane):
    inside = pl.ds(ZP, nz)
    for k in range(2):
        ref[0, half + 2 + k, inside] = jnp.where(lane < 64, pltpu.roll(ref[0, 2 + k, inside], 64, 1), 0.0)
        ref[0, k, inside] = jnp.where(lane >= 64, pltpu.roll(ref[0, half + k, inside], 64, 1), 0.0)


def bands():
    def weight(distance):
        return {1: -16.0, 2: 1.0}.get(abs(distance), 0.0)

    block = np.array([[weight(i - j) for j in range(128)] for i in range(128)], np.float32)
    sections = np.zeros((2, 6, 128, 2, 128), np.float32)
    for h in range(2):
        for c in range(2):
            ends = np.zeros((128, 128), np.float32)
            for i in range(HALO):
                for j in range(128):
                    ends[64 * h + 32 * c + i, j] = weight(i - HALO - j)
                    ends[64 * h + 32 * c + 16 + HALO + i, j] = weight(128 + i - j)
            for piece in range(2):
                sections[h, 2 * piece + c, :, c] = block
                sections[h, 4 + piece, :, c] = ends
    halo = np.zeros((2, 128, 128), np.float32)
    for start in range(0, 128, 16):
        halo[:, start : start + 2 * HALO, start : start + 2 * HALO] = block[: 2 * HALO, : 2 * HALO]
    return jnp.asarray(sections.reshape(2, 768, 256), jnp.bfloat16), jnp.asarray(halo.reshape(256, 128), jnp.bfloat16)


def split(pieces, value, row, first, second):
    rows = pl.ds(pl.multiple_of(row, 16), value.shape[0])
    high = value.astype(jnp.bfloat16)
    pieces[rows, 128 * first : 128 * (first + 1)] = high
    rest = (value - high.astype(jnp.float32)).astype(jnp.bfloat16)
    pieces[rows, 128 * second : 128 * (second + 1)] = rest


def begin_kernel(psi, trial, own_ends, *refs):
    rounds, ny, nz, _ = psi.shape
    columns = trial.shape[0]
    lane = lanes(nz)
    for r in range(rounds):
        w, u, v, pieces = refs[4 * r : 4 * r + 4]
        for ref in (w, u, v):
            clear_borders(ref, nz, (0, 1, ny + 2, ny + 3))

        @pl.loop(0, ny)
        def _(y):
            for z in range(0, nz, CHUNK):
                here = psi[r, y, pl.ds(z, CHUNK)]
                for c in range(columns):
                    value = here * trial[c, y, pl.ds(z, CHUNK)]
                    w[c, y + 2, pl.ds(ZP + z, CHUNK)] = value
                    split(pieces, value, y * nz + z, c, 2 + c)

        for y in range(ny // 2):
            own_ends[r, y] = inner_lanes(psi[r, y], psi[r, y + ny // 2], lane)


def main_scratch(rounds, ny, nz, nx):
    half = ny // 2
    return (
        [pltpu.VMEM((1, half + 4, nz + 2 * ZP, nx), jnp.float32)] * (3 * rounds)
        + [pltpu.VMEM((ny * nz, 2 * nx), jnp.float32)] * rounds
        + [pltpu.VMEM((half * nz, nx), jnp.float32)]
    )


def main_kernel(rounds, psi, left, right, trial_halo, scaled, scaled_halo, bands, halo_bands, own_ends, *refs):
    given, refs = refs[: 4 * rounds], refs[4 * rounds :]
    out, changed, refs = refs[0], refs[1 : 1 + 3 * rounds], refs[1 + 3 * rounds :]
    arrays = [ref for r in range(rounds) for ref in (given[4 * r], *changed[3 * r : 3 * r + 3])]
    halos, sums, halo_sums = refs[: 3 * rounds], refs[3 * rounds : 4 * rounds], refs[4 * rounds]
    columns, ny, nz, _ = out.shape
    half = ny // 2
    full = lanes(nz)
    blocks = ny // DEPTH

    def multiply(r, block):
        rows = pl.ds(pl.multiple_of(block * (DEPTH * nz), 16), DEPTH * nz)
        matrix = bands[block // (blocks // 2)]
        sums[r][rows, :] = jnp.dot(arrays[4 * r + 3][rows, :], matrix, preferred_element_type=jnp.float32)

    def put_halo(r, target, y, z, value):
        target[0, y + 2, pl.ds(ZP + z, value.shape[0])] = value
        for h in range(2):
            split(arrays[4 * r + 3], value, (y + h * half) * nz + z, 4, 5)

    def start(r):
        for ref in halos[3 * r : 3 * r + 3]:
            clear_borders(ref, nz, ())
        for y in range(half):
            part = outer_lanes(left[r], right[r], full, y) + own_ends[r, y]
            put_halo(r, halos[3 * r], y, 0, (part + pltpu.roll(part, 32, 1)) * trial_halo[y])
        wrap_halo(halos[3 * r], half, nz, full)

    def halo_stage(r, step, shift, weight):
        first, source, target = halos[3 * r], halos[3 * r + step], halos[3 * r + step + 1]
        halo_sums[...] = jnp.dot(
            arrays[4 * r + 3][: half * nz, 512:], halo_bands[...], preferred_element_type=jnp.float32
        )

        @pl.loop(0, half)
        def _(y):
            for z in range(0, nz, CHUNK):
                rows = pl.ds(ZP + z, CHUNK)
                f = source[0, y + 2, rows]
                near, far = rows_around(source, 0, y + 2, ZP + z, CHUNK)
                near = near + (source[0, y + 1, rows] + source[0, y + 3, rows])
                far = far + (source[0, y, rows] + source[0, y + 4, rows])
                along = halo_sums[pl.ds(pl.multiple_of(y * nz + z, CHUNK), CHUNK), :]
                value = (far + along) - 16.0 * near + (scaled_halo[y, pl.ds(z, CHUNK)] - shift) * f
                if weight:
                    value = value - weight * first[0, y + 2, rows]
                put_halo(r, target, y, z, value)

        wrap_halo(target, half, nz, full)

    def stage(r, step, shift, weight, beside):
        first, source = arrays[4 * r], arrays[4 * r + step]

        @pl.loop(0, blocks)
        def _(block):
            if beside is not None:
                multiply(beside, block)
            for z in range(0, nz, SHORT):
                rows = pl.ds(ZP + z, SHORT)
                for c in range(columns):
                    planes = [source[c, block * DEPTH + k, rows] for k in range(DEPTH + 4)]
                    for k in range(DEPTH):
                        y = block * DEPTH + k
                        near, far = rows_around(source, c, y + 2, ZP + z, SHORT)
                        near = near + (planes[k + 1] + planes[k + 3])
                        far = far + (planes[k] + planes[k + 4])
                        along = sums[r][pl.ds(pl.multiple_of(y * nz + z, SHORT), SHORT), 128 * c : 128 * (c + 1)]
                        diagonal = scaled[y, pl.ds(z, SHORT)]
                        if shift:
                            diagonal = diagonal - shift
                        value = (far + along) - 16.0 * near + diagonal * planes[k + 2]
                        if weight:
                            value = value - weight * first[c, y + 2, rows]
                        if step < 2:
                            arrays[4 * r + step + 1][c, y + 2, rows] = value
                            split(arrays[4 * r + 3], value, y * nz + z, c, 2 + c)
                        else:
                            term = (FINAL * psi[r, y, pl.ds(z, SHORT)]) * value
                            if r:
                                term = term + out[c, y, pl.ds(z, SHORT)]
                            out[c, y, pl.ds(z, SHORT)] = term

    steps = ((ALPHA, None), (0.0, BETA), (0.0, GAMMA))
    turns = [(step, r) for step in range(3) for r in range(rounds)]
    for r in range(rounds):
        start(r)

    @pl.loop(0, blocks)
    def _(block):
        multiply(0, block)

    for at, (step, r) in enumerate(turns):
        if step < 2:
            halo_stage(r, step, *steps[step])
        stage(r, step, *steps[step], turns[at + 1][1] if at + 1 < len(turns) else None)


def vmem(count):
    return [pl.BlockSpec(memory_space=pltpu.VMEM)] * count


def params(mib):
    return pltpu.CompilerParams(vmem_limit_bytes=mib << 20)


def f32(*shape):
    return jax.ShapeDtypeStruct(shape, jnp.float32)


def exchange(pieces):
    n = pieces.shape[0]
    if n > 16:
        arranged = jnp.take(pieces, lax.axis_index("cols") ^ jnp.arange(n), axis=0)
        got = lax.all_to_all(arranged, "cols", 0, 0)
        return [got[s : s + 1] for s in range(n)]
    got = {0: pieces[:1]}
    reach = 1 << (n - 1).bit_length() - 1
    for group in ([k for k in range(reach, n)], [k for k in range(1, reach)]):
        sent = [pieces[k : k + 1] for k in group]
        pieces, *sent = lax.optimization_barrier([pieces, *sent])
        for k, piece in sorted(zip(group, sent), key=lambda pair: (-pair[0].bit_length(), pair[0] & 1, pair[0])):
            got[k] = lax.ppermute(piece, "cols", [(i, i ^ k) for i in range(n)])
    return [got[k] for k in range(n)]


def pick_kernel(owner, *refs):
    got, own = refs[:-1], refs[-1]
    me = lax.axis_index("cols") if len(got) <= 16 else 0
    for r in range(own.shape[0]):
        for k, piece in enumerate(got):

            @pl.when((me ^ owner[r]) == k)
            def _():
                own[r] = piece[0]


def cost(mib):
    return pl.CostEstimate(flops=0, transcendentals=0, bytes_accessed=mib << 20)


def body(trial, orbitals, potential, owner):
    columns, ny, nz, nx = trial.shape
    n, parts = lax.axis_size("cols"), lax.axis_size("sec")
    rounds = owner.shape[0]
    rows = ny * nz // n
    sec_up = [(i, (i + 1) % parts) for i in range(parts)]
    sec_down = [(j, i) for i, j in sec_up]

    got = exchange(orbitals.reshape(n, rows, nx))
    last, first = pl.pallas_call(
        pack_kernel,
        out_shape=[f32(columns + 1, nz, nx)] * 2,
        in_specs=vmem(2),
        out_specs=vmem(2),
        compiler_params=params(8),
        cost_estimate=cost(6),
    )(trial, potential)
    left = lax.ppermute(last, "sec", sec_up)
    right = lax.ppermute(first, "sec", sec_down)
    prepared = pl.pallas_call(
        prepare_kernel,
        out_shape=[f32(ny // 2, nz, nx), f32(ny, nz, nx), f32(ny // 2, nz, nx)],
        in_specs=vmem(4),
        out_specs=vmem(3),
        compiler_params=params(10),
        cost_estimate=cost(10),
    )(trial, potential, left, right)
    trial_halo, scaled, scaled_halo = prepared

    ring = ring_of(n)
    clockwise = [(ring[i], ring[(i + 1) % n]) for i in range(n)]
    counter = [(j, i) for i, j in clockwise]
    smem = [pl.BlockSpec(memory_space=pltpu.SMEM)]
    own = pl.pallas_call(
        pick_kernel,
        out_shape=f32(rounds, rows, nx),
        in_specs=smem + vmem(n),
        out_specs=pl.BlockSpec(memory_space=pltpu.VMEM),
        compiler_params=params(4),
        name="pick",
    )(owner, *got)
    ahead = behind = own
    blocks = [own]
    for step in range(1, n // 2 + 1):
        if 2 * step == n:
            cut = rows // 16 * 8
            ahead, behind = ahead[:, :cut], behind[:, cut:]
        ahead = lax.ppermute(ahead, "cols", clockwise)
        behind = lax.ppermute(behind, "cols", counter)
        blocks += [ahead, behind]

    psi, psi_last, psi_first = pl.pallas_call(
        functools.partial(gather_kernel, n, rounds),
        out_shape=[f32(rounds, ny * nz, nx), f32(rounds, nz, nx), f32(rounds, nz, nx)],
        in_specs=smem + vmem(len(blocks)),
        out_specs=vmem(3),
        compiler_params=params(10),
        name="gather",
    )(owner, *blocks)
    psi = psi.reshape(rounds, ny, nz, nx)
    psi_left = lax.ppermute(psi_last, "sec", sec_up)
    psi_right = lax.ppermute(psi_first, "sec", sec_down)
    padded = f32(columns, ny + 4, nz + 2 * ZP, nx)
    pieces = jax.ShapeDtypeStruct((ny * nz, 6 * nx), jnp.bfloat16)
    own_ends, *arrays = pl.pallas_call(
        begin_kernel,
        out_shape=[f32(rounds, ny // 2, nz, nx)] + [padded, padded, padded, pieces] * rounds,
        in_specs=vmem(2),
        out_specs=vmem(1 + 4 * rounds),
        compiler_params=params(20),
        cost_estimate=cost(8),
    )(psi, trial)
    given = [psi, psi_left, psi_right, trial_halo, scaled, scaled_halo, *bands(), own_ends, *arrays]
    changed = [len(given) - 4 * rounds + 4 * r + k for r in range(rounds) for k in (1, 2, 3)]
    return pl.pallas_call(
        functools.partial(main_kernel, rounds),
        out_shape=[f32(columns, ny, nz, nx)] + [padded, padded, pieces] * rounds,
        in_specs=vmem(len(given)),
        out_specs=vmem(1 + 3 * rounds),
        input_output_aliases={i: 1 + k for k, i in enumerate(changed)},
        scratch_shapes=main_scratch(rounds, ny, nz, nx),
        compiler_params=params(20),
        name="main",
    )(*given)[0]


def solution(mesh):
    placed = (P("cols", None, None, "sec"), P("cols", None, None, "sec"), P(None, None, "sec"), P())

    return jax.shard_map(body, mesh=mesh, in_specs=placed, out_specs=P("cols", None, None, "sec"), check_vma=False)
```

```python
import functools

import jax
import jax.numpy as jnp
import numpy as np
from jax import lax
from jax.experimental import pallas as pl
from jax.experimental.pallas import tpu as pltpu
from jax.sharding import PartitionSpec as P

SCALE = 120.0
ALPHA = 0.6 * SCALE
BETA = 0.25 * SCALE**2
GAMMA = 0.1 * SCALE**3
FINAL = -2.0 / SCALE**3
HALO = 6
ZP = 8
CHUNK = 32
SHORT = 16
DEPTH = 8


def lanes(rows):
    return lax.broadcasted_iota(jnp.int32, (rows, 128), 1)


def between(lane, low, high):
    return (lane >= low) & (lane < high)


def pack_edges(plane, ny, lane, first):
    tile = jnp.zeros_like(plane(0))
    for y in range(ny):
        source = 0 if first else 128 - HALO
        moved = pltpu.roll(plane(y), (8 * y - source) % 128, 1)
        tile = jnp.where(between(lane, 8 * y, 8 * y + HALO), moved, tile)
    return tile


def outer_lanes(left, right, lane, y):
    inner = lane % 64
    tile = jnp.where(inner < 6, pltpu.roll(left, (-8 * y) % 128, 1), 0.0)
    return jnp.where(between(inner, 22, 28), pltpu.roll(right, (22 - 8 * y) % 128, 1), tile)


def inner_lanes(low, high, lane):
    tile = jnp.where(between(lane, 6, 12), pltpu.roll(low, 6, 1), 0.0)
    tile = jnp.where(between(lane, 16, 22), pltpu.roll(low, 22, 1), tile)
    tile = jnp.where(between(lane, 70, 76), pltpu.roll(high, 70, 1), tile)
    return jnp.where(between(lane, 80, 86), pltpu.roll(high, 86, 1), tile)


def halo_plane(left, right, low, high, lane, y):
    return outer_lanes(left, right, lane, y) + inner_lanes(low, high, lane)


def pack_kernel(trial, potential, last, first):
    columns, ny, nz, _ = trial.shape
    lane = lanes(nz)
    for out, leading in ((last, False), (first, True)):
        for c in range(columns):
            out[c] = pack_edges(lambda y: trial[c, y], ny, lane, leading)
        out[columns] = pack_edges(lambda y: potential[y], ny, lane, leading)


def prepare_kernel(trial, potential, left, right, trial_halo, scaled, scaled_halo):
    columns, ny, nz, _ = trial.shape
    lane = lanes(nz)
    half = ny // 2
    for y in range(half):
        tile = jnp.zeros((nz, 128), jnp.float32)
        for c in range(columns):
            part = halo_plane(left[c], right[c], trial[c, y], trial[c, y + half], lane, y)
            tile = tile + (pltpu.roll(part, 32 * c, 1) if c else part)
        trial_halo[y] = tile
        part = halo_plane(left[columns], right[columns], potential[y], potential[y + half], lane, y)
        scaled_halo[y] = 6.0 * (part + pltpu.roll(part, 32, 1)) - 6.0
    for y in range(ny):
        scaled[y] = 6.0 * potential[y] - 6.0


def ring_of(n):
    return [*range(0, n, 2), *range(n - 1 - n % 2, 0, -2)]


def gather_kernel(n, rounds, owner, *refs):
    blocks, (whole, last, first) = refs[:-3], refs[-3:]
    nz = last.shape[1]
    ny = whole.shape[1] // nz
    evens = (n + 1) // 2
    me = lax.axis_index("cols")
    spot = jnp.where(me % 2 == 0, me // 2, n - 1 - me // 2)
    rows = blocks[0].shape[1]

    def put(block, shift, last_part):
        position = lax.rem(spot + shift + n, n)
        device = jnp.where(position < evens, 2 * position, 2 * (n - 1 - position) + 1)
        size = block.shape[1]
        for r in range(rounds):
            start = (device ^ owner[r]) * rows + (rows - size if last_part else 0)
            whole[r, pl.ds(pl.multiple_of(start, 8), size), :] = block[r]

    put(blocks[0], 0, False)
    for k, block in enumerate(blocks[1:]):
        step, ahead = k // 2 + 1, k % 2 == 0
        put(block, -step if ahead else step, not ahead)
    lane = lanes(nz)
    for r in range(rounds):
        last[r] = pack_edges(lambda y: whole[r, y * nz : (y + 1) * nz], ny, lane, False)
        first[r] = pack_edges(lambda y: whole[r, y * nz : (y + 1) * nz], ny, lane, True)


def clear_borders(ref, nz, planes):
    zero = jnp.zeros((ZP, 128), jnp.float32)
    for c in range(ref.shape[0]):
        for y in range(ref.shape[1]):
            if y in planes:
                ref[c, y] = jnp.zeros_like(ref[c, y])
            else:
                ref[c, y, 0:ZP] = zero
                ref[c, y, ZP + nz : 2 * ZP + nz] = zero


def rows_around(ref, c, y, at, rows):
    near = ref[c, y, pl.ds(at - 1, rows)] + ref[c, y, pl.ds(at + 1, rows)]
    far = ref[c, y, pl.ds(at - 2, rows)] + ref[c, y, pl.ds(at + 2, rows)]
    return near, far


def wrap_halo(ref, half, nz, lane):
    inside = pl.ds(ZP, nz)
    for k in range(2):
        ref[0, half + 2 + k, inside] = jnp.where(lane < 64, pltpu.roll(ref[0, 2 + k, inside], 64, 1), 0.0)
        ref[0, k, inside] = jnp.where(lane >= 64, pltpu.roll(ref[0, half + k, inside], 64, 1), 0.0)


def bands():
    def weight(distance):
        return {1: -16.0, 2: 1.0}.get(abs(distance), 0.0)

    block = np.array([[weight(i - j) for j in range(128)] for i in range(128)], np.float32)
    sections = np.zeros((2, 6, 128, 2, 128), np.float32)
    for h in range(2):
        for c in range(2):
            ends = np.zeros((128, 128), np.float32)
            for i in range(HALO):
                for j in range(128):
                    ends[64 * h + 32 * c + i, j] = weight(i - HALO - j)
                    ends[64 * h + 32 * c + 16 + HALO + i, j] = weight(128 + i - j)
            for piece in range(2):
                sections[h, 2 * piece + c, :, c] = block
                sections[h, 4 + piece, :, c] = ends
    halo = np.zeros((2, 128, 128), np.float32)
    for start in range(0, 128, 16):
        halo[:, start : start + 2 * HALO, start : start + 2 * HALO] = block[: 2 * HALO, : 2 * HALO]
    return jnp.asarray(sections.reshape(2, 768, 256), jnp.bfloat16), jnp.asarray(halo.reshape(256, 128), jnp.bfloat16)


def split(pieces, value, row, first, second):
    rows = pl.ds(pl.multiple_of(row, 16), value.shape[0])
    high = value.astype(jnp.bfloat16)
    pieces[rows, 128 * first : 128 * (first + 1)] = high
    rest = (value - high.astype(jnp.float32)).astype(jnp.bfloat16)
    pieces[rows, 128 * second : 128 * (second + 1)] = rest


def begin_kernel(psi, trial, own_ends, *refs):
    rounds, ny, nz, _ = psi.shape
    columns = trial.shape[0]
    lane = lanes(nz)
    for r in range(rounds):
        w, u, v, pieces = refs[4 * r : 4 * r + 4]
        for ref in (w, u, v):
            clear_borders(ref, nz, (0, 1, ny + 2, ny + 3))

        @pl.loop(0, ny)
        def _(y):
            for z in range(0, nz, CHUNK):
                here = psi[r, y, pl.ds(z, CHUNK)]
                for c in range(columns):
                    value = here * trial[c, y, pl.ds(z, CHUNK)]
                    w[c, y + 2, pl.ds(ZP + z, CHUNK)] = value
                    split(pieces, value, y * nz + z, c, 2 + c)

        for y in range(ny // 2):
            own_ends[r, y] = inner_lanes(psi[r, y], psi[r, y + ny // 2], lane)


def main_scratch(rounds, ny, nz, nx):
    half = ny // 2
    return (
        [pltpu.VMEM((1, half + 4, nz + 2 * ZP, nx), jnp.float32)] * (3 * rounds)
        + [pltpu.VMEM((ny * nz, 2 * nx), jnp.float32)] * rounds
        + [pltpu.VMEM((half * nz, nx), jnp.float32)]
    )


def main_kernel(rounds, psi, left, right, trial_halo, scaled, scaled_halo, bands, halo_bands, own_ends, *refs):
    given, refs = refs[: 4 * rounds], refs[4 * rounds :]
    out, changed, refs = refs[0], refs[1 : 1 + 3 * rounds], refs[1 + 3 * rounds :]
    arrays = [ref for r in range(rounds) for ref in (given[4 * r], *changed[3 * r : 3 * r + 3])]
    halos, sums, halo_sums = refs[: 3 * rounds], refs[3 * rounds : 4 * rounds], refs[4 * rounds]
    columns, ny, nz, _ = out.shape
    half = ny // 2
    full = lanes(nz)
    blocks = ny // DEPTH

    def multiply(r, block):
        rows = pl.ds(pl.multiple_of(block * (DEPTH * nz), 16), DEPTH * nz)
        matrix = bands[block // (blocks // 2)]
        sums[r][rows, :] = jnp.dot(arrays[4 * r + 3][rows, :], matrix, preferred_element_type=jnp.float32)

    def put_halo(r, target, y, z, value):
        target[0, y + 2, pl.ds(ZP + z, value.shape[0])] = value
        for h in range(2):
            split(arrays[4 * r + 3], value, (y + h * half) * nz + z, 4, 5)

    def start(r):
        for ref in halos[3 * r : 3 * r + 3]:
            clear_borders(ref, nz, ())
        for y in range(half):
            part = outer_lanes(left[r], right[r], full, y) + own_ends[r, y]
            put_halo(r, halos[3 * r], y, 0, (part + pltpu.roll(part, 32, 1)) * trial_halo[y])
        wrap_halo(halos[3 * r], half, nz, full)

    def halo_stage(r, step, shift, weight):
        first, source, target = halos[3 * r], halos[3 * r + step], halos[3 * r + step + 1]
        halo_sums[...] = jnp.dot(
            arrays[4 * r + 3][: half * nz, 512:], halo_bands[...], preferred_element_type=jnp.float32
        )

        @pl.loop(0, half // 4)
        def _(block):
            for z in range(0, nz, SHORT):
                rows = pl.ds(ZP + z, SHORT)
                planes = [source[0, 4 * block + k, rows] for k in range(8)]
                for k in range(4):
                    y = 4 * block + k
                    near, far = rows_around(source, 0, y + 2, ZP + z, SHORT)
                    near = near + (planes[k + 1] + planes[k + 3])
                    far = far + (planes[k] + planes[k + 4])
                    along = halo_sums[pl.ds(pl.multiple_of(y * nz + z, SHORT), SHORT), :]
                    diagonal = scaled_halo[y, pl.ds(z, SHORT)]
                    if shift:
                        diagonal = diagonal - shift
                    value = (far + along) - 16.0 * near + diagonal * planes[k + 2]
                    if weight:
                        value = value - weight * first[0, y + 2, rows]
                    put_halo(r, target, y, z, value)

        wrap_halo(target, half, nz, full)

    def stage(r, step, shift, weight, beside):
        first, source = arrays[4 * r], arrays[4 * r + step]

        @pl.loop(0, blocks)
        def _(block):
            if beside is not None:
                multiply(beside, block)
            for z in range(0, nz, SHORT):
                rows = pl.ds(ZP + z, SHORT)
                for c in range(columns):
                    planes = [source[c, block * DEPTH + k, rows] for k in range(DEPTH + 4)]
                    for k in range(DEPTH):
                        y = block * DEPTH + k
                        near, far = rows_around(source, c, y + 2, ZP + z, SHORT)
                        near = near + (planes[k + 1] + planes[k + 3])
                        far = far + (planes[k] + planes[k + 4])
                        along = sums[r][pl.ds(pl.multiple_of(y * nz + z, SHORT), SHORT), 128 * c : 128 * (c + 1)]
                        diagonal = scaled[y, pl.ds(z, SHORT)]
                        if shift:
                            diagonal = diagonal - shift
                        value = (far + along) - 16.0 * near + diagonal * planes[k + 2]
                        if weight:
                            value = value - weight * first[c, y + 2, rows]
                        if step < 2:
                            arrays[4 * r + step + 1][c, y + 2, rows] = value
                            split(arrays[4 * r + 3], value, y * nz + z, c, 2 + c)
                        else:
                            term = (FINAL * psi[r, y, pl.ds(z, SHORT)]) * value
                            if r:
                                term = term + out[c, y, pl.ds(z, SHORT)]
                            out[c, y, pl.ds(z, SHORT)] = term

    steps = ((ALPHA, None), (0.0, BETA), (0.0, GAMMA))
    turns = [(step, r) for step in range(3) for r in range(rounds)]
    start(0)
    for block in range(blocks):
        multiply(0, block)
    for r in range(1, rounds):
        start(r)

    for at, (step, r) in enumerate(turns):
        if step < 2:
            halo_stage(r, step, *steps[step])
        stage(r, step, *steps[step], turns[at + 1][1] if at + 1 < len(turns) else None)


def vmem(count):
    return [pl.BlockSpec(memory_space=pltpu.VMEM)] * count


def params(mib):
    return pltpu.CompilerParams(vmem_limit_bytes=mib << 20)


def f32(*shape):
    return jax.ShapeDtypeStruct(shape, jnp.float32)


def exchange(pieces):
    n = pieces.shape[0]
    if n > 16:
        arranged = jnp.take(pieces, lax.axis_index("cols") ^ jnp.arange(n), axis=0)
        got = lax.all_to_all(arranged, "cols", 0, 0)
        return [got[s : s + 1] for s in range(n)]
    got = {0: pieces[:1]}
    reach = 1 << (n - 1).bit_length() - 1
    for group in ([k for k in range(reach, n)], [k for k in range(1, reach)]):
        sent = [pieces[k : k + 1] for k in group]
        pieces, *sent = lax.optimization_barrier([pieces, *sent])
        for k, piece in sorted(zip(group, sent), key=lambda pair: (-pair[0].bit_length(), pair[0] & 1, pair[0])):
            got[k] = lax.ppermute(piece, "cols", [(i, i ^ k) for i in range(n)])
    return [got[k] for k in range(n)]


def pick_kernel(owner, *refs):
    got, own = refs[:-1], refs[-1]
    me = lax.axis_index("cols") if len(got) <= 16 else 0
    for r in range(own.shape[0]):
        for k, piece in enumerate(got):

            @pl.when((me ^ owner[r]) == k)
            def _():
                own[r] = piece[0]


def cost(mib):
    return pl.CostEstimate(flops=0, transcendentals=0, bytes_accessed=mib << 20)


def body(trial, orbitals, potential, owner):
    columns, ny, nz, nx = trial.shape
    n, parts = lax.axis_size("cols"), lax.axis_size("sec")
    rounds = owner.shape[0]
    rows = ny * nz // n
    sec_up = [(i, (i + 1) % parts) for i in range(parts)]
    sec_down = [(j, i) for i, j in sec_up]

    got = exchange(orbitals.reshape(n, rows, nx))
    last, first = pl.pallas_call(
        pack_kernel,
        out_shape=[f32(columns + 1, nz, nx)] * 2,
        in_specs=vmem(2),
        out_specs=vmem(2),
        compiler_params=params(8),
        cost_estimate=cost(6),
    )(trial, potential)
    left = lax.ppermute(last, "sec", sec_up)
    right = lax.ppermute(first, "sec", sec_down)
    prepared = pl.pallas_call(
        prepare_kernel,
        out_shape=[f32(ny // 2, nz, nx), f32(ny, nz, nx), f32(ny // 2, nz, nx)],
        in_specs=vmem(4),
        out_specs=vmem(3),
        compiler_params=params(10),
        cost_estimate=cost(10),
    )(trial, potential, left, right)
    trial_halo, scaled, scaled_halo = prepared

    ring = ring_of(n)
    clockwise = [(ring[i], ring[(i + 1) % n]) for i in range(n)]
    counter = [(j, i) for i, j in clockwise]
    smem = [pl.BlockSpec(memory_space=pltpu.SMEM)]
    own = pl.pallas_call(
        pick_kernel,
        out_shape=f32(rounds, rows, nx),
        in_specs=smem + vmem(n),
        out_specs=pl.BlockSpec(memory_space=pltpu.VMEM),
        compiler_params=params(4),
        name="pick",
    )(owner, *got)
    ahead = behind = own
    blocks = [own]
    for step in range(1, n // 2 + 1):
        if 2 * step == n:
            cut = rows // 16 * 8
            ahead, behind = ahead[:, :cut], behind[:, cut:]
        ahead = lax.ppermute(ahead, "cols", clockwise)
        behind = lax.ppermute(behind, "cols", counter)
        blocks += [ahead, behind]

    psi, psi_last, psi_first = pl.pallas_call(
        functools.partial(gather_kernel, n, rounds),
        out_shape=[f32(rounds, ny * nz, nx), f32(rounds, nz, nx), f32(rounds, nz, nx)],
        in_specs=smem + vmem(len(blocks)),
        out_specs=vmem(3),
        compiler_params=params(10),
        name="gather",
    )(owner, *blocks)
    psi = psi.reshape(rounds, ny, nz, nx)
    psi_left = lax.ppermute(psi_last, "sec", sec_up)
    psi_right = lax.ppermute(psi_first, "sec", sec_down)
    padded = f32(columns, ny + 4, nz + 2 * ZP, nx)
    pieces = jax.ShapeDtypeStruct((ny * nz, 6 * nx), jnp.bfloat16)
    own_ends, *arrays = pl.pallas_call(
        begin_kernel,
        out_shape=[f32(rounds, ny // 2, nz, nx)] + [padded, padded, padded, pieces] * rounds,
        in_specs=vmem(2),
        out_specs=vmem(1 + 4 * rounds),
        compiler_params=params(20),
        cost_estimate=cost(8),
    )(psi, trial)
    given = [psi, psi_left, psi_right, trial_halo, scaled, scaled_halo, *bands(), own_ends, *arrays]
    changed = [len(given) - 4 * rounds + 4 * r + k for r in range(rounds) for k in (1, 2, 3)]
    return pl.pallas_call(
        functools.partial(main_kernel, rounds),
        out_shape=[f32(columns, ny, nz, nx)] + [padded, padded, pieces] * rounds,
        in_specs=vmem(len(given)),
        out_specs=vmem(1 + 3 * rounds),
        input_output_aliases={i: 1 + k for k, i in enumerate(changed)},
        scratch_shapes=main_scratch(rounds, ny, nz, nx),
        compiler_params=params(20),
        name="main",
    )(*given)[0]


def solution(mesh):
    placed = (P("cols", None, None, "sec"), P("cols", None, None, "sec"), P(None, None, "sec"), P())

    return jax.shard_map(body, mesh=mesh, in_specs=placed, out_specs=P("cols", None, None, "sec"), check_vma=False)
```

```python
import functools

import jax
import jax.numpy as jnp
import numpy as np
from jax import lax
from jax.experimental import pallas as pl
from jax.experimental.pallas import tpu as pltpu
from jax.sharding import PartitionSpec as P

SCALE = 120.0
ALPHA = 0.6 * SCALE
BETA = 0.25 * SCALE**2
GAMMA = 0.1 * SCALE**3
FINAL = -2.0 / SCALE**3
HALO = 6
ZP = 8
CHUNK = 32
SHORT = 16
DEPTH = 8


def lanes(rows):
    return lax.broadcasted_iota(jnp.int32, (rows, 128), 1)


def between(lane, low, high):
    return (lane >= low) & (lane < high)


def pack_edges(plane, ny, lane, first):
    tile = jnp.zeros_like(plane(0))
    for y in range(ny):
        source = 0 if first else 128 - HALO
        moved = pltpu.roll(plane(y), (8 * y - source) % 128, 1)
        tile = jnp.where(between(lane, 8 * y, 8 * y + HALO), moved, tile)
    return tile


def outer_lanes(left, right, lane, y):
    inner = lane % 64
    tile = jnp.where(inner < 6, pltpu.roll(left, (-8 * y) % 128, 1), 0.0)
    return jnp.where(between(inner, 22, 28), pltpu.roll(right, (22 - 8 * y) % 128, 1), tile)


def inner_lanes(low, high, lane):
    tile = jnp.where(between(lane, 6, 12), pltpu.roll(low, 6, 1), 0.0)
    tile = jnp.where(between(lane, 16, 22), pltpu.roll(low, 22, 1), tile)
    tile = jnp.where(between(lane, 70, 76), pltpu.roll(high, 70, 1), tile)
    return jnp.where(between(lane, 80, 86), pltpu.roll(high, 86, 1), tile)


def halo_plane(left, right, low, high, lane, y):
    return outer_lanes(left, right, lane, y) + inner_lanes(low, high, lane)


def pack_kernel(trial, potential, last, first):
    columns, ny, nz, _ = trial.shape
    lane = lanes(nz)
    for out, leading in ((last, False), (first, True)):
        for c in range(columns):
            out[c] = pack_edges(lambda y: trial[c, y], ny, lane, leading)
        out[columns] = pack_edges(lambda y: potential[y], ny, lane, leading)


def prepare_kernel(trial, potential, left, right, trial_halo, scaled, scaled_halo):
    columns, ny, nz, _ = trial.shape
    lane = lanes(nz)
    half = ny // 2
    for y in range(half):
        tile = jnp.zeros((nz, 128), jnp.float32)
        for c in range(columns):
            part = halo_plane(left[c], right[c], trial[c, y], trial[c, y + half], lane, y)
            tile = tile + (pltpu.roll(part, 32 * c, 1) if c else part)
        trial_halo[y] = tile
        part = halo_plane(left[columns], right[columns], potential[y], potential[y + half], lane, y)
        scaled_halo[y] = 6.0 * (part + pltpu.roll(part, 32, 1)) - 6.0
    for y in range(ny):
        scaled[y] = 6.0 * potential[y] - 6.0


def ring_of(n):
    return [*range(0, n, 2), *range(n - 1 - n % 2, 0, -2)]


def gather_kernel(n, rounds, owner, *refs):
    blocks, (whole, last, first) = refs[:-3], refs[-3:]
    nz = last.shape[1]
    ny = whole.shape[1] // nz
    evens = (n + 1) // 2
    me = lax.axis_index("cols")
    spot = jnp.where(me % 2 == 0, me // 2, n - 1 - me // 2)
    rows = blocks[0].shape[1]

    def put(block, shift, last_part):
        position = lax.rem(spot + shift + n, n)
        device = jnp.where(position < evens, 2 * position, 2 * (n - 1 - position) + 1)
        size = block.shape[1]
        for r in range(rounds):
            start = (device ^ owner[r]) * rows + (rows - size if last_part else 0)
            whole[r, pl.ds(pl.multiple_of(start, 8), size), :] = block[r]

    put(blocks[0], 0, False)
    for k, block in enumerate(blocks[1:]):
        step, ahead = k // 2 + 1, k % 2 == 0
        put(block, -step if ahead else step, not ahead)
    lane = lanes(nz)
    for r in range(rounds):
        last[r] = pack_edges(lambda y: whole[r, y * nz : (y + 1) * nz], ny, lane, False)
        first[r] = pack_edges(lambda y: whole[r, y * nz : (y + 1) * nz], ny, lane, True)


def clear_borders(ref, nz, planes):
    zero = jnp.zeros((ZP, 128), jnp.float32)
    for c in range(ref.shape[0]):
        for y in range(ref.shape[1]):
            if y in planes:
                ref[c, y] = jnp.zeros_like(ref[c, y])
            else:
                ref[c, y, 0:ZP] = zero
                ref[c, y, ZP + nz : 2 * ZP + nz] = zero


def rows_around(ref, c, y, at, rows):
    near = ref[c, y, pl.ds(at - 1, rows)] + ref[c, y, pl.ds(at + 1, rows)]
    far = ref[c, y, pl.ds(at - 2, rows)] + ref[c, y, pl.ds(at + 2, rows)]
    return near, far


def wrap_halo(ref, half, nz, lane):
    inside = pl.ds(ZP, nz)
    for k in range(2):
        ref[0, half + 2 + k, inside] = jnp.where(lane < 64, pltpu.roll(ref[0, 2 + k, inside], 64, 1), 0.0)
        ref[0, k, inside] = jnp.where(lane >= 64, pltpu.roll(ref[0, half + k, inside], 64, 1), 0.0)


def bands():
    def weight(distance):
        return {1: -16.0, 2: 1.0}.get(abs(distance), 0.0)

    block = np.array([[weight(i - j) for j in range(128)] for i in range(128)], np.float32)
    sections = np.zeros((2, 6, 128, 2, 128), np.float32)
    for h in range(2):
        for c in range(2):
            ends = np.zeros((128, 128), np.float32)
            for i in range(HALO):
                for j in range(128):
                    ends[64 * h + 32 * c + i, j] = weight(i - HALO - j)
                    ends[64 * h + 32 * c + 16 + HALO + i, j] = weight(128 + i - j)
            for piece in range(2):
                sections[h, 2 * piece + c, :, c] = block
                sections[h, 4 + piece, :, c] = ends
    halo = np.zeros((2, 128, 128), np.float32)
    for start in range(0, 128, 16):
        halo[:, start : start + 2 * HALO, start : start + 2 * HALO] = block[: 2 * HALO, : 2 * HALO]
    return jnp.asarray(sections.reshape(2, 768, 256), jnp.bfloat16), jnp.asarray(halo.reshape(256, 128), jnp.bfloat16)


def split(pieces, value, row, first, second):
    rows = pl.ds(pl.multiple_of(row, 16), value.shape[0])
    high = value.astype(jnp.bfloat16)
    pieces[rows, 128 * first : 128 * (first + 1)] = high
    rest = (value - high.astype(jnp.float32)).astype(jnp.bfloat16)
    pieces[rows, 128 * second : 128 * (second + 1)] = rest


def begin_kernel(psi, trial, own_ends, *refs):
    rounds, ny, nz, _ = psi.shape
    columns = trial.shape[0]
    lane = lanes(nz)
    for r in range(rounds):
        w, u, v, pieces = refs[4 * r : 4 * r + 4]
        for ref in (w, u, v):
            clear_borders(ref, nz, (0, 1, ny + 2, ny + 3))

        @pl.loop(0, ny)
        def _(y):
            for z in range(0, nz, CHUNK):
                here = psi[r, y, pl.ds(z, CHUNK)]
                for c in range(columns):
                    value = here * trial[c, y, pl.ds(z, CHUNK)]
                    w[c, y + 2, pl.ds(ZP + z, CHUNK)] = value
                    split(pieces, value, y * nz + z, c, 2 + c)

        for y in range(ny // 2):
            own_ends[r, y] = inner_lanes(psi[r, y], psi[r, y + ny // 2], lane)


def main_scratch(rounds, ny, nz, nx):
    half = ny // 2
    return (
        [pltpu.VMEM((1, half + 4, nz + 2 * ZP, nx), jnp.float32)] * (3 * rounds)
        + [pltpu.VMEM((ny * nz, 2 * nx), jnp.float32)] * rounds
        + [pltpu.VMEM((half * nz, nx), jnp.float32)]
    )


def main_kernel(rounds, psi, left, right, trial_halo, scaled, scaled_halo, bands, halo_bands, own_ends, *refs):
    given, refs = refs[: 4 * rounds], refs[4 * rounds :]
    out, changed, refs = refs[0], refs[1 : 1 + 3 * rounds], refs[1 + 3 * rounds :]
    arrays = [ref for r in range(rounds) for ref in (given[4 * r], *changed[3 * r : 3 * r + 3])]
    halos, sums, halo_sums = refs[: 3 * rounds], refs[3 * rounds : 4 * rounds], refs[4 * rounds]
    columns, ny, nz, _ = out.shape
    half = ny // 2
    full = lanes(nz)
    blocks = ny // DEPTH

    def multiply(r, block):
        rows = pl.ds(pl.multiple_of(block * (DEPTH * nz), 16), DEPTH * nz)
        matrix = bands[block // (blocks // 2)]
        sums[r][rows, :] = jnp.dot(arrays[4 * r + 3][rows, :], matrix, preferred_element_type=jnp.float32)

    def put_halo(r, target, y, z, value):
        target[0, y + 2, pl.ds(ZP + z, value.shape[0])] = value
        for h in range(2):
            split(arrays[4 * r + 3], value, (y + h * half) * nz + z, 4, 5)

    def start(r):
        for ref in halos[3 * r : 3 * r + 3]:
            clear_borders(ref, nz, ())
        for y in range(half):
            part = outer_lanes(left[r], right[r], full, y) + own_ends[r, y]
            put_halo(r, halos[3 * r], y, 0, (part + pltpu.roll(part, 32, 1)) * trial_halo[y])
        wrap_halo(halos[3 * r], half, nz, full)

    def halo_stage(r, step, shift, weight):
        first, source, target = halos[3 * r], halos[3 * r + step], halos[3 * r + step + 1]
        halo_sums[...] = jnp.dot(
            arrays[4 * r + 3][: half * nz, 512:], halo_bands[...], preferred_element_type=jnp.float32
        )

        @pl.loop(0, half // 4)
        def _(block):
            for z in range(0, nz, SHORT):
                rows = pl.ds(ZP + z, SHORT)
                planes = [source[0, 4 * block + k, rows] for k in range(8)]
                for k in range(4):
                    y = 4 * block + k
                    near, far = rows_around(source, 0, y + 2, ZP + z, SHORT)
                    near = near + (planes[k + 1] + planes[k + 3])
                    far = far + (planes[k] + planes[k + 4])
                    along = halo_sums[pl.ds(pl.multiple_of(y * nz + z, SHORT), SHORT), :]
                    diagonal = scaled_halo[y, pl.ds(z, SHORT)]
                    if shift:
                        diagonal = diagonal - shift
                    value = (far + along) - 16.0 * near + diagonal * planes[k + 2]
                    if weight:
                        value = value - weight * first[0, y + 2, rows]
                    put_halo(r, target, y, z, value)

        wrap_halo(target, half, nz, full)

    def stage(r, step, shift, weight, beside):
        first, source = arrays[4 * r], arrays[4 * r + step]

        @pl.loop(0, blocks)
        def _(block):
            if beside is not None:
                multiply(beside, block)
            for z in range(0, nz, SHORT):
                rows = pl.ds(ZP + z, SHORT)
                for c in range(columns):
                    planes = [source[c, block * DEPTH + k, rows] for k in range(DEPTH + 4)]
                    for k in range(DEPTH):
                        y = block * DEPTH + k
                        near, far = rows_around(source, c, y + 2, ZP + z, SHORT)
                        near = near + (planes[k + 1] + planes[k + 3])
                        far = far + (planes[k] + planes[k + 4])
                        along = sums[r][pl.ds(pl.multiple_of(y * nz + z, SHORT), SHORT), 128 * c : 128 * (c + 1)]
                        diagonal = scaled[y, pl.ds(z, SHORT)]
                        if shift:
                            diagonal = diagonal - shift
                        value = (far + along) - 16.0 * near + diagonal * planes[k + 2]
                        if weight:
                            value = value - weight * first[c, y + 2, rows]
                        if step < 2:
                            arrays[4 * r + step + 1][c, y + 2, rows] = value
                            split(arrays[4 * r + 3], value, y * nz + z, c, 2 + c)
                        else:
                            term = (FINAL * psi[r, y, pl.ds(z, SHORT)]) * value
                            if r:
                                term = term + out[c, y, pl.ds(z, SHORT)]
                            out[c, y, pl.ds(z, SHORT)] = term

    steps = ((ALPHA, None), (0.0, BETA), (0.0, GAMMA))
    turns = [(step, r) for step in range(3) for r in range(rounds)]
    start(0)
    for block in range(blocks):
        multiply(0, block)
    for r in range(1, rounds):
        start(r)

    for at, (step, r) in enumerate(turns):
        if step < 2:
            halo_stage(r, step, *steps[step])
        stage(r, step, *steps[step], turns[at + 1][1] if at + 1 < len(turns) else None)


def vmem(count):
    return [pl.BlockSpec(memory_space=pltpu.VMEM)] * count


def params(mib):
    return pltpu.CompilerParams(vmem_limit_bytes=mib << 20)


def f32(*shape):
    return jax.ShapeDtypeStruct(shape, jnp.float32)


def exchange(pieces):
    n = pieces.shape[0]
    if n > 16:
        arranged = jnp.take(pieces, lax.axis_index("cols") ^ jnp.arange(n), axis=0)
        got = lax.all_to_all(arranged, "cols", 0, 0)
        return [got[s : s + 1] for s in range(n)]
    got = {0: pieces[:1]}
    reach = 1 << (n - 1).bit_length() - 1
    far = range(reach, n)
    close = sorted(range(1, reach), key=lambda k: (-k.bit_length(), k & 1, k))
    for group in ([k for k in far if k % 2 == 0], [k for k in far if k % 2], close):
        sent = [pieces[k : k + 1] for k in group]
        pieces, *sent = lax.optimization_barrier([pieces, *sent])
        for k, piece in zip(group, sent):
            got[k] = lax.ppermute(piece, "cols", [(i, i ^ k) for i in range(n)])
    return [got[k] for k in range(n)]


def pick_kernel(owner, *refs):
    got, own = refs[:-1], refs[-1]
    me = lax.axis_index("cols") if len(got) <= 16 else 0
    for r in range(own.shape[0]):
        for k, piece in enumerate(got):

            @pl.when((me ^ owner[r]) == k)
            def _():
                own[r] = piece[0]


def cost(mib):
    return pl.CostEstimate(flops=0, transcendentals=0, bytes_accessed=mib << 20)


def body(trial, orbitals, potential, owner):
    columns, ny, nz, nx = trial.shape
    n, parts = lax.axis_size("cols"), lax.axis_size("sec")
    rounds = owner.shape[0]
    rows = ny * nz // n
    sec_up = [(i, (i + 1) % parts) for i in range(parts)]
    sec_down = [(j, i) for i, j in sec_up]

    got = exchange(orbitals.reshape(n, rows, nx))
    last, first = pl.pallas_call(
        pack_kernel,
        out_shape=[f32(columns + 1, nz, nx)] * 2,
        in_specs=vmem(2),
        out_specs=vmem(2),
        compiler_params=params(8),
        cost_estimate=cost(6),
    )(trial, potential)
    left = lax.ppermute(last, "sec", sec_up)
    right = lax.ppermute(first, "sec", sec_down)
    prepared = pl.pallas_call(
        prepare_kernel,
        out_shape=[f32(ny // 2, nz, nx), f32(ny, nz, nx), f32(ny // 2, nz, nx)],
        in_specs=vmem(4),
        out_specs=vmem(3),
        compiler_params=params(10),
        cost_estimate=cost(10),
    )(trial, potential, left, right)
    trial_halo, scaled, scaled_halo = prepared

    ring = ring_of(n)
    clockwise = [(ring[i], ring[(i + 1) % n]) for i in range(n)]
    counter = [(j, i) for i, j in clockwise]
    smem = [pl.BlockSpec(memory_space=pltpu.SMEM)]
    own = pl.pallas_call(
        pick_kernel,
        out_shape=f32(rounds, rows, nx),
        in_specs=smem + vmem(n),
        out_specs=pl.BlockSpec(memory_space=pltpu.VMEM),
        compiler_params=params(4),
        name="pick",
    )(owner, *got)
    ahead = behind = own
    blocks = [own]
    for step in range(1, n // 2 + 1):
        if 2 * step == n:
            cut = rows // 16 * 8
            ahead, behind = ahead[:, :cut], behind[:, cut:]
        ahead = lax.ppermute(ahead, "cols", clockwise)
        behind = lax.ppermute(behind, "cols", counter)
        blocks += [ahead, behind]

    psi, psi_last, psi_first = pl.pallas_call(
        functools.partial(gather_kernel, n, rounds),
        out_shape=[f32(rounds, ny * nz, nx), f32(rounds, nz, nx), f32(rounds, nz, nx)],
        in_specs=smem + vmem(len(blocks)),
        out_specs=vmem(3),
        compiler_params=params(10),
        name="gather",
    )(owner, *blocks)
    psi = psi.reshape(rounds, ny, nz, nx)
    psi_left = lax.ppermute(psi_last, "sec", sec_up)
    psi_right = lax.ppermute(psi_first, "sec", sec_down)
    padded = f32(columns, ny + 4, nz + 2 * ZP, nx)
    pieces = jax.ShapeDtypeStruct((ny * nz, 6 * nx), jnp.bfloat16)
    own_ends, *arrays = pl.pallas_call(
        begin_kernel,
        out_shape=[f32(rounds, ny // 2, nz, nx)] + [padded, padded, padded, pieces] * rounds,
        in_specs=vmem(2),
        out_specs=vmem(1 + 4 * rounds),
        compiler_params=params(20),
        cost_estimate=cost(8),
    )(psi, trial)
    given = [psi, psi_left, psi_right, trial_halo, scaled, scaled_halo, *bands(), own_ends, *arrays]
    changed = [len(given) - 4 * rounds + 4 * r + k for r in range(rounds) for k in (1, 2, 3)]
    return pl.pallas_call(
        functools.partial(main_kernel, rounds),
        out_shape=[f32(columns, ny, nz, nx)] + [padded, padded, pieces] * rounds,
        in_specs=vmem(len(given)),
        out_specs=vmem(1 + 3 * rounds),
        input_output_aliases={i: 1 + k for k, i in enumerate(changed)},
        scratch_shapes=main_scratch(rounds, ny, nz, nx),
        compiler_params=params(20),
        name="main",
    )(*given)[0]


def solution(mesh):
    placed = (P("cols", None, None, "sec"), P("cols", None, None, "sec"), P(None, None, "sec"), P())

    return jax.shard_map(body, mesh=mesh, in_specs=placed, out_specs=P("cols", None, None, "sec"), check_vma=False)
```
